32 devices in a mesh: dp: 8 (over z, x), row: 2 (over y), col: 2 (over core).
Axes of the slice: x: 2, y: 2, z: 4, core: 2. Of those that a mesh axis runs over, the one named last changes fastest.
Arguments:
- block_input: bfloat16 [6272, 512], P('dp', 'row'), may hold values from -6 to 6
- out_grad: bfloat16 [6272, 512], P('dp', 'row'), may hold values from -6 to 6
- first_gain: float32 [512], P('row'), may hold values from 0.5 to 1.5
- first_shift: float32 [512], P('row'), may hold values from -3 to 3
- qkv_weight: bfloat16 [512, 3, 512], P('row', None, 'col'), may hold values from -0.25 to 0.25
- query_bias: float32 [512], P('col'), may hold values from -3 to 3
- value_bias: float32 [512], P('col'), may hold values from -0.6 to 0.6
- position_table: float32 [169, 16], P(None, 'col'), may hold values from -6 to 306
- position_index: int32 [49, 49], replicated, may hold values from 0 to 168
- proj_weight: bfloat16 [512, 512], P('col', 'row'), may hold values from -2 to 2
- proj_bias: float32 [512], P('row'), may hold values from -1.2 to 1.2
- second_gain: float32 [512], P('row'), may hold values from 0.5 to 1.5
- second_shift: float32 [512], P('row'), may hold values from -3 to 3
- expand_weight: bfloat16 [512, 2048], P('row', 'col'), may hold values from -0.5 to 0.5
- expand_bias: float32 [2048], P('col'), may hold values from -3 to 3
- reduce_weight: bfloat16 [2048, 512], P('col', 'row'), may hold values from -0.5 to 0.5
- reduce_bias: float32 [512], P('row'), may hold values from -3 to 3
Outputs:
- block_output: bfloat16 [6272, 512], P('dp', 'row')
- input_grad: float32 [6272, 512], P('dp', 'row')
- first_gain_grad: float32 [512], P('row')
- first_shift_grad: float32 [512], P('row')
- qkv_weight_grad: float32 [512, 3, 512], P('row', None, 'col')
- query_bias_grad: float32 [512], P('col')
- value_bias_grad: float32 [512], P('col')
- position_table_grad: float32 [169, 16], P(None, 'col')
- proj_weight_grad: float32 [512, 512], P('col', 'row')
- proj_bias_grad: float32 [512], P('row')
- second_gain_grad: float32 [512], P('row')
- second_shift_grad: float32 [512], P('row')
- expand_weight_grad: float32 [512, 2048], P('row', 'col')
- expand_bias_grad: float32 [2048], P('col')
- reduce_weight_grad: float32 [2048, 512], P('col', 'row')
- reduce_bias_grad: float32 [512], P('row')
The draws below stay inside these ranges and needn't reach their ends.
Inputs may be any that keep to these rules, and one draw needn't show every extreme that they name: `position_index`: entries name rows of position_table.
All inputs are finite; a program needn't handle non-finite values.
Results may differ from the reference program's by a relative error of at most 0.012.
The reference program's roundings to bfloat16 on the way count: a program that leaves them out, or rounds other values in their place, can miss the bound.
Values may be sent and summed in bfloat16 or wider, within the bound.
A program may use at most 64 MiB of HBM per device.

```python
import math
import jax
import jax.numpy as jnp
from jax import lax

WIDTH = 512
HEADS = 16
MLP_WIDTH = 2048
WINDOW = 49
TABLE = 169
TOKENS = 6272


def draw_position_table(key, part):
    base_key = jax.random.fold_in(key, 0)
    table = jnp.clip(jax.random.normal(base_key, (TABLE, HEADS), jnp.float32), -6.0, 6.0)
    return table


def set_ends(drawn, own_key, low, top_value):
    spot = [jax.random.randint(jax.random.fold_in(own_key, axis), (), 0, length) for axis, length in enumerate(drawn.shape)]
    longest = drawn.shape.index(max(drawn.shape))
    beside = spot[:longest] + [(spot[longest] + 1) % drawn.shape[longest]] + spot[longest + 1:]
    return drawn.at[tuple(spot)].set(low).at[tuple(beside)].set(top_value)


def shard_levels(own_key, extent, cuts, least, high):
    loudness, own = 1.0, jax.random.fold_in(own_key, 6)
    for position, shards_of in cuts:
        heights = jnp.exp(jax.random.uniform(jax.random.fold_in(own, position), (shards_of,), jnp.float32, least / len(cuts), high / len(cuts)))
        loudness = loudness * jnp.repeat(heights, extent[position] // shards_of).reshape([-1 if axis == position else 1 for axis in range(len(extent))])
    return loudness


def noise(rng, dims, scale, bound, cuts=(), dtype=jnp.bfloat16):
    factor_of = shard_levels(rng, dims, cuts, -0.22, 0.18) if cuts else 1.0
    values = jax.random.normal(rng, dims, jnp.float32) * scale * factor_of
    return jnp.minimum(jnp.maximum(values, -bound), bound).astype(dtype)


def setup_inputs(seed: int = 0) -> dict:
    key_of = jax.random.split(jax.random.key(seed), 18)
    block_input = noise(key_of[0], (TOKENS, WIDTH), 1.0, 6.0, ((0, 8), (1, 2)))
    out_grad = noise(key_of[1], (TOKENS, WIDTH), 1.0, 6.0, ((0, 8), (1, 2)))
    first_gain = jnp.clip(1.0 + 0.1 * jax.random.normal(key_of[2], (WIDTH,), jnp.float32), 0.5, 1.5)
    first_shift = noise(key_of[3], (WIDTH,), 0.5, 3.0, ((0, 2),), jnp.float32)
    qkv_weight = noise(key_of[4], (WIDTH, 3, WIDTH), WIDTH ** -0.5, 0.25, ((0, 2), (2, 2)))
    query_bias = noise(key_of[5], (WIDTH,), 0.5, 3.0, ((0, 2),), jnp.float32)
    value_bias = noise(key_of[6], (WIDTH,), 0.1, 0.6, ((0, 2),), jnp.float32)
    position_table = draw_position_table(jax.random.fold_in(key_of[17], 71), 0)
    position_index = set_ends(jax.random.randint(key_of[8], (WINDOW, WINDOW), 0, TABLE), jax.random.fold_in(key_of[8], 1), 0, TABLE - 1).astype(jnp.int32)
    proj_weight = noise(key_of[9], (WIDTH, WIDTH), (WIDTH // 49) ** -0.5, 2.0, ((0, 2), (1, 2)))
    proj_bias = noise(key_of[10], (WIDTH,), 0.2, 1.2, ((0, 2),), jnp.float32)
    second_gain = jnp.clip(1.0 + 0.1 * jax.random.normal(key_of[11], (WIDTH,), jnp.float32), 0.5, 1.5)
    second_shift = noise(key_of[12], (WIDTH,), 0.5, 3.0, ((0, 2),), jnp.float32)
    expand_weight = noise(key_of[13], (WIDTH, MLP_WIDTH), (WIDTH // 4) ** -0.5, 0.5, ((0, 2), (1, 2)))
    expand_bias = noise(key_of[14], (MLP_WIDTH,), 0.5, 3.0, ((0, 2),), jnp.float32)
    reduce_weight = noise(key_of[15], (MLP_WIDTH, WIDTH), (MLP_WIDTH // 16) ** -0.5, 0.5, ((0, 2), (1, 2)))
    reduce_bias = noise(key_of[16], (WIDTH,), 0.5, 3.0, ((0, 2),), jnp.float32)
    return dict(block_input=block_input, out_grad=out_grad, first_gain=first_gain, first_shift=first_shift, qkv_weight=qkv_weight, query_bias=query_bias, value_bias=value_bias, position_table=position_table, position_index=position_index, proj_weight=proj_weight, proj_bias=proj_bias, second_gain=second_gain, second_shift=second_shift, expand_weight=expand_weight, expand_bias=expand_bias, reduce_weight=reduce_weight, reduce_bias=reduce_bias)


EPSILON = 1e-05
ROOT_HALF = 0.7071067811865476
GAUSS_PEAK = 0.3989422804014327

def rounded(tensor):
    return lax.optimization_barrier(tensor.astype(jnp.bfloat16))

def to_windows(tokens):
    features = tokens.shape[-1]
    halves = tokens.shape[0] // 98
    shaped = tokens.reshape(halves, 7, 2, 7, features).transpose(0, 2, 1, 3, 4)
    return shaped.reshape(halves * 2, 49, features)

def from_windows(windows):
    features = windows.shape[-1]
    halves = windows.shape[0] // 2
    shaped = windows.reshape(halves, 2, 7, 7, features).transpose(0, 2, 1, 3, 4)
    return shaped.reshape(halves * 98, features)

def split_heads(tokens, head_count):
    windows = to_windows(tokens)
    return windows.reshape(windows.shape[0], 49, head_count, windows.shape[2] // head_count)

def merge_heads(windows):
    merged = windows.reshape(windows.shape[0], 49, windows.shape[2] * windows.shape[3])
    return from_windows(merged)

def gelu_value(pre_act):
    return 0.5 * pre_act * (1.0 + jax.scipy.special.erf(pre_act * ROOT_HALF))

def gelu_slope(pre_act):
    return 0.5 * (1.0 + jax.scipy.special.erf(pre_act * ROOT_HALF)) + pre_act * GAUSS_PEAK * jnp.exp(-0.5 * pre_act * pre_act)

def norm_forward(values):
    center = lax.optimization_barrier(jnp.mean(values, axis=-1, keepdims=True))
    shifted = values - center
    spread = lax.optimization_barrier(jnp.mean(shifted * shifted, axis=-1, keepdims=True))
    inverse = lax.rsqrt(spread + EPSILON)
    return (shifted * inverse, inverse)

def norm_backward(upstream, gain, normed, inverse):
    scaled = upstream * gain
    grad_mean = lax.optimization_barrier(jnp.mean(scaled, axis=-1, keepdims=True))
    grad_corr = lax.optimization_barrier(jnp.mean(scaled * normed, axis=-1, keepdims=True))
    return inverse * (scaled - grad_mean - normed * grad_corr)

def layer_block(block_rows, grad_rows, weights, pos_bias):
    first_gain, first_shift, qkv_weight, query_bias, value_bias, proj_weight, proj_bias, second_gain, second_shift, expand_weight, expand_bias, reduce_weight, reduce_bias = weights
    full_width = block_rows.shape[1]
    head_count = pos_bias.shape[0]
    score_scale = (full_width // head_count) ** (-0.5)
    inputs = block_rows.astype(jnp.float32)
    normed_one, inverse_one = norm_forward(inputs)
    ln_one = rounded(normed_one * first_gain + first_shift)
    flat_weight = qkv_weight.reshape(full_width, 3 * full_width)
    linear = jnp.dot(ln_one, flat_weight, preferred_element_type=jnp.float32).reshape(-1, 3, full_width)
    bias_rows = jnp.stack([query_bias, jnp.zeros_like(query_bias), value_bias])
    linear = linear + bias_rows[None]
    queries = rounded(linear[:, 0] * score_scale)
    key_rows = rounded(linear[:, 1])
    value_rows = rounded(linear[:, 2])
    query_heads = split_heads(queries, head_count).astype(jnp.float32)
    key_heads = split_heads(key_rows, head_count).astype(jnp.float32)
    value_heads = split_heads(value_rows, head_count).astype(jnp.float32)
    scores = jnp.einsum('wihd,wjhd->whij', query_heads, key_heads) + pos_bias[None]
    row_top = lax.optimization_barrier(jnp.max(scores, axis=-1, keepdims=True))
    log_total = row_top + jnp.log(lax.optimization_barrier(jnp.sum(jnp.exp(scores - row_top), axis=-1, keepdims=True)))
    probs = jnp.exp(scores - log_total)
    probs_b = rounded(probs).astype(jnp.float32)
    mixed = rounded(merge_heads(jnp.einsum('whij,wjhd->wihd', probs_b, value_heads)))
    middle = inputs + jnp.dot(mixed, proj_weight, preferred_element_type=jnp.float32) + proj_bias
    normed_two, inverse_two = norm_forward(middle)
    ln_two = rounded(normed_two * second_gain + second_shift)
    pre_act = jnp.dot(ln_two, expand_weight, preferred_element_type=jnp.float32) + expand_bias
    hidden = rounded(gelu_value(pre_act))
    block_out = (middle + jnp.dot(hidden, reduce_weight, preferred_element_type=jnp.float32) + reduce_bias).astype(jnp.bfloat16)
    upstream = grad_rows.astype(jnp.float32)
    reduce_w_grad = jnp.dot(hidden.T, grad_rows, preferred_element_type=jnp.float32)
    reduce_b_grad = lax.optimization_barrier(jnp.sum(upstream, axis=0))
    hidden_grad = jnp.dot(grad_rows, reduce_weight.T, preferred_element_type=jnp.float32)
    pre_grad = rounded(hidden_grad * gelu_slope(pre_act))
    expand_b_grad = lax.optimization_barrier(jnp.sum(pre_grad.astype(jnp.float32), axis=0))
    expand_w_grad = jnp.dot(ln_two.T, pre_grad, preferred_element_type=jnp.float32)
    second_grad = jnp.dot(pre_grad, expand_weight.T, preferred_element_type=jnp.float32)
    second_gain_grad = lax.optimization_barrier(jnp.sum(second_grad * normed_two, axis=0))
    second_shift_grad = lax.optimization_barrier(jnp.sum(second_grad, axis=0))
    middle_grad = upstream + norm_backward(second_grad, second_gain, normed_two, inverse_two)
    middle_b = rounded(middle_grad)
    proj_w_grad = jnp.dot(mixed.T, middle_b, preferred_element_type=jnp.float32)
    proj_b_grad = lax.optimization_barrier(jnp.sum(middle_grad, axis=0))
    mixed_grad = rounded(jnp.dot(middle_b, proj_weight.T, preferred_element_type=jnp.float32))
    grad_heads = split_heads(mixed_grad, head_count).astype(jnp.float32)
    prob_grad = jnp.einsum('wihd,wjhd->whij', grad_heads, value_heads)
    value_grad = jnp.einsum('whij,wihd->wjhd', probs_b, grad_heads)
    centre = lax.optimization_barrier(jnp.sum(probs * prob_grad, axis=-1, keepdims=True))
    score_grad = probs * (prob_grad - centre)
    bias_grad = lax.optimization_barrier(jnp.sum(score_grad, axis=0))
    score_b = rounded(score_grad).astype(jnp.float32)
    query_grad = jnp.einsum('whij,wjhd->wihd', score_b, key_heads) * score_scale
    key_grad = jnp.einsum('whij,wihd->wjhd', score_b, query_heads)
    linear_grad = jnp.stack([merge_heads(query_grad), merge_heads(key_grad), merge_heads(value_grad)], axis=1)
    query_b_grad = lax.optimization_barrier(jnp.sum(linear_grad[:, 0], axis=0))
    value_b_grad = lax.optimization_barrier(jnp.sum(linear_grad[:, 2], axis=0))
    linear_b = rounded(linear_grad).reshape(-1, 3 * full_width)
    qkv_grad = jnp.dot(ln_one.T, linear_b, preferred_element_type=jnp.float32).reshape(full_width, 3, full_width)
    first_grad = jnp.dot(linear_b, flat_weight.T, preferred_element_type=jnp.float32)
    first_gain_grad = lax.optimization_barrier(jnp.sum(first_grad * normed_one, axis=0))
    first_shift_grad = lax.optimization_barrier(jnp.sum(first_grad, axis=0))
    input_grad = middle_grad + norm_backward(first_grad, first_gain, normed_one, inverse_one)
    grads = (first_gain_grad, first_shift_grad, qkv_grad, query_b_grad, value_b_grad, bias_grad, proj_w_grad, proj_b_grad, second_gain_grad, second_shift_grad, expand_w_grad, expand_b_grad, reduce_w_grad, reduce_b_grad)
    return (block_out, input_grad, grads)

def reference(block_input, out_grad, first_gain, first_shift, qkv_weight, query_bias, value_bias, position_table, position_index, proj_weight, proj_bias, second_gain, second_shift, expand_weight, expand_bias, reduce_weight, reduce_bias):
    weights = (first_gain, first_shift, qkv_weight, query_bias, value_bias, proj_weight, proj_bias, second_gain, second_shift, expand_weight, expand_bias, reduce_weight, reduce_bias)
    pos_bias = position_table[position_index].transpose(2, 0, 1)
    images = block_input.shape[0] // 196
    group_size = math.gcd(images, 16)
    block_rows = group_size * 196
    block_count = images // group_size
    inputs = block_input.reshape(block_count, block_rows, block_input.shape[1])
    grads_in = out_grad.reshape(block_count, block_rows, out_grad.shape[1])
    zero_grads = tuple((jnp.zeros(tensor.shape, jnp.float32) for tensor in weights[:5])) + (jnp.zeros(pos_bias.shape, jnp.float32),) + tuple((jnp.zeros(tensor.shape, jnp.float32) for tensor in weights[5:]))

    def one_block(totals, sample):
        block_out, input_grad, grads = layer_block(sample[0], sample[1], weights, pos_bias)
        return (jax.tree.map(jnp.add, totals, grads), (block_out, input_grad))
    total_grads, (outputs, input_grads) = lax.scan(one_block, zero_grads, (inputs, grads_in))
    head_count = position_table.shape[1]
    table_grad = jnp.zeros(position_table.shape, jnp.float32).at[position_index.reshape(-1)].add(total_grads[5].transpose(1, 2, 0).reshape(-1, head_count))
    return (outputs.reshape(block_input.shape), input_grads.reshape(block_input.shape), total_grads[0], total_grads[1], total_grads[2], total_grads[3], total_grads[4], table_grad, total_grads[6], total_grads[7], total_grads[8], total_grads[9], total_grads[10], total_grads[11], total_grads[12], total_grads[13])
```

```python
import functools

import jax
import jax.numpy as jnp
import numpy as np
from jax import lax
from jax.experimental import pallas as pl
from jax.experimental.pallas import tpu as pltpu
from jax.sharding import PartitionSpec as P

EPSILON = 1e-05
ROOT_HALF = 0.7071067811865476
GAUSS_PEAK = 0.3989422804014327
SIDE = 7
WINDOW = SIDE * SIDE
IMAGE = 4 * WINDOW
PAD = 64
ROWS = 4 * PAD
F32 = jnp.float32
BF16 = jnp.bfloat16
VMEM = pl.BlockSpec(memory_space=pltpu.VMEM)
MESH = pl.DeviceIdType.MESH
LIMIT = 60 * 1024 * 1024


def permutation():
    table = np.zeros((ROWS, IMAGE), np.float32)
    for window in range(4):
        for i in range(WINDOW):
            row = window // 2 * SIDE + i // SIDE
            column = window % 2 * SIDE + i % SIDE
            table[window * PAD + i, row * 2 * SIDE + column] = 1.0
    return table


def dot(left, right):
    return jnp.dot(left, right, preferred_element_type=F32)


def dot_t(left, right):
    return lax.dot_general(left, right, (((1,), (1,)), ((), ())), preferred_element_type=F32)


def t_dot(left, right):
    return lax.dot_general(left, right, (((0,), (0,)), ((), ())), preferred_element_type=F32)


def norm(values):
    center = jnp.mean(values, axis=-1, keepdims=True)
    shifted = values - center
    spread = jnp.mean(shifted * shifted, axis=-1, keepdims=True)
    inverse = lax.rsqrt(spread + EPSILON)
    return shifted * inverse, inverse


def norm_backward(upstream, gain, normed, inverse):
    scaled = upstream * gain
    return inverse * (
        scaled
        - jnp.mean(scaled, axis=-1, keepdims=True)
        - normed * jnp.mean(scaled * normed, axis=-1, keepdims=True)
    )


def head_mask(heads, width):
    size = width // heads
    head = lax.broadcasted_iota(jnp.int32, (heads, 1, width), 0)
    lane = lax.broadcasted_iota(jnp.int32, (heads, 1, width), 2)
    return (lane >= head * size) & (lane < (head + 1) * size)


def stack_heads(rows, mask):
    heads = mask.shape[0]
    wide = jnp.where(mask, rows.astype(F32)[None], 0.0)
    return wide.reshape(heads * rows.shape[0], rows.shape[1]).astype(BF16)


def fold_heads(stacked, mask):
    heads = mask.shape[0]
    split = stacked.reshape(heads, stacked.shape[0] // heads, stacked.shape[1])
    return jnp.sum(jnp.where(mask, split, 0.0), axis=0)


def softmax(scores):
    top = jnp.max(scores, axis=-1, keepdims=True)
    total = top + jnp.log(jnp.sum(jnp.exp(scores - top), axis=-1, keepdims=True))
    return jnp.exp(scores - total)


def attend_kernel(
    perm, x_own, x_oth, rvec, qb, vb, bias, w_oo, w_xo, w_ox, w_xx, p_oo, p_xo, p_ox, p_xx,
    q_out, k_out, v_out, mixed_out, middle_out, x_out,
):
    half = x_own.shape[1]
    width = p_oo.shape[0]
    heads = bias.shape[1] // PAD
    size = width // heads
    scale = size ** (-0.5)
    x = dot(perm[...], jnp.concatenate([x_own[...], x_oth[...]], axis=1))
    x_out[...] = x.astype(BF16)
    normed, _ = norm(x)
    ln = (normed * rvec[0:1] + rvec[1:2]).astype(BF16)
    mask = head_mask(heads, width)
    for b, (w_own, w_oth) in enumerate(((w_oo, w_xo), (w_ox, w_xx))):
        cols = slice(b * width, (b + 1) * width)
        for s, out in enumerate((q_out, k_out, v_out)):
            part = slice(s * width, (s + 1) * width)
            linear = dot(ln[:, :half], w_own[:, part]) + dot(ln[:, half:], w_oth[:, part])
            if s == 0:
                linear = (linear + qb[:, cols]) * scale
            if s == 2:
                linear = linear + vb[:, cols]
            out[:, cols] = linear.astype(BF16)

        def window(w, carry):
            rows = pl.ds(pl.multiple_of(w * PAD, PAD), PAD)
            scores = dot_t(stack_heads(q_out[rows, cols], mask), k_out[rows, cols]) + bias[b]
            probs = softmax(scores).astype(BF16)
            mixed_out[rows, cols] = fold_heads(dot(probs, v_out[rows, cols]), mask).astype(BF16)
            return carry

        lax.fori_loop(0, 4, window, 0)
    for a, (p_own, p_oth) in enumerate(((p_oo, p_ox), (p_xo, p_xx))):
        cols = slice(a * half, (a + 1) * half)
        middle_out[:, cols] = (
            x[:, cols]
            + (dot(mixed_out[:, :width], p_own[...]) + dot(mixed_out[:, width:], p_oth[...]))
            + rvec[2:3, cols]
        )


def mlp_kernel(
    perm, g_own, g_oth, rvec, eb, middle_ref, e_oo, e_xo, e_ox, e_xx, r_oo, r_xo, r_ox, r_xx,
    out_ref, mgrad_ref, o_ref, x_ref, y_ref, z_ref, rsum_ref, ebg_ref,
    pre_ref, hidden_ref, pg_ref,
):
    half = g_own.shape[1]
    hid = e_oo.shape[1]
    middle = middle_ref[...]
    normed, inverse = norm(middle)
    ln = (normed * rvec[3:4] + rvec[4:5]).astype(BF16)
    grad = dot(perm[...], jnp.concatenate([g_own[...], g_oth[...]], axis=1))
    grad_b = grad.astype(BF16)
    for b, (e_own, e_oth, r_own, r_oth, own_w, oth_w) in enumerate(
        ((e_oo, e_xo, r_oo, r_xo, o_ref, x_ref), (e_ox, e_xx, r_ox, r_xx, y_ref, z_ref))
    ):
        for q in range(hid // half):
            here = slice(q * half, (q + 1) * half)
            cols = slice(b * hid + q * half, b * hid + (q + 1) * half)
            pre = dot(ln[:, :half], e_own[:, here]) + dot(ln[:, half:], e_oth[:, here])
            pre = pre + eb[:, cols]
            erf_half = 0.5 * (1.0 + lax.erf(pre * ROOT_HALF))
            hidden = (pre * erf_half).astype(BF16)
            hidden_ref[:, cols] = hidden
            slope = erf_half + pre * GAUSS_PEAK * jnp.exp(-0.5 * pre * pre)
            hgrad = dot_t(grad_b[:, :half], r_own[here, :]) + dot_t(grad_b[:, half:], r_oth[here, :])
            pgrad = (hgrad * slope).astype(BF16)
            pg_ref[:, cols] = pgrad
            ebg_ref[:, cols] = jnp.sum(pgrad.astype(F32), axis=0, keepdims=True)
            own_w[here, :] = t_dot(ln[:, :half], pgrad).astype(own_w.dtype)
            oth_w[here, :] = t_dot(ln[:, half:], pgrad).astype(oth_w.dtype)
            down = slice(hid + q * half, hid + (q + 1) * half)
            own_w[down, :] = t_dot(hidden, grad_b[:, :half]).astype(own_w.dtype)
            oth_w[down, :] = t_dot(hidden, grad_b[:, half:]).astype(oth_w.dtype)
    parts, grads = [], []
    for r_a, r_b, e_a, e_b in ((r_oo, r_ox, e_oo, e_ox), (r_xo, r_xx, e_xo, e_xx)):
        parts.append(dot(hidden_ref[:, :hid], r_a[...]) + dot(hidden_ref[:, hid:], r_b[...]))
        grads.append(dot_t(pg_ref[:, :hid], e_a[...]) + dot_t(pg_ref[:, hid:], e_b[...]))
    block = (middle + jnp.concatenate(parts, axis=1) + rvec[5:6]).astype(BF16)
    out_ref[...] = t_dot(perm[...], block).astype(BF16)
    second = jnp.concatenate(grads, axis=1)
    mgrad = grad + norm_backward(second, rvec[3:4], normed, inverse)
    mgrad_ref[...] = mgrad
    rsum_ref[...] = jnp.zeros_like(rsum_ref)
    rsum_ref[0:1] = jnp.sum(mgrad, axis=0, keepdims=True)
    rsum_ref[1:2] = jnp.sum(second * normed, axis=0, keepdims=True)
    rsum_ref[2:3] = jnp.sum(second, axis=0, keepdims=True)
    rsum_ref[3:4] = jnp.sum(grad, axis=0, keepdims=True)


def back_kernel(
    perm, x_ref, q_ref, k_ref, v_ref, mixed_ref, mgrad_ref, rvec, bias,
    w_oo, w_xo, w_ox, w_xx, p_oo, p_xo, p_ox, p_xx,
    in_ref, o_ref, xx_ref, y_ref, z_ref, rsum_ref, qvsum_ref, bgrad_ref,
    mg_ref, lin_ref,
):
    width = p_oo.shape[0]
    half = p_oo.shape[1]
    heads = bias.shape[1] // PAD
    scale = (width // heads) ** (-0.5)
    normed, inverse = norm(x_ref[...].astype(F32))
    ln = (normed * rvec[0:1] + rvec[1:2]).astype(BF16)
    mgrad = mgrad_ref[...]
    middle_b = mgrad.astype(BF16)
    mask = head_mask(heads, width)
    bgrad_ref[...] = jnp.zeros_like(bgrad_ref)
    qvsum_ref[...] = jnp.zeros_like(qvsum_ref)
    first = [jnp.zeros((ROWS, half), F32), jnp.zeros((ROWS, half), F32)]
    for b, (p_own, p_oth, w_own, w_oth, own_w, oth_w) in enumerate(
        ((p_oo, p_xo, w_oo, w_xo, o_ref, xx_ref), (p_ox, p_xx, w_ox, w_xx, y_ref, z_ref))
    ):
        cols = slice(b * width, (b + 1) * width)
        mg_ref[:, cols] = (
            dot_t(middle_b[:, :half], p_own[...]) + dot_t(middle_b[:, half:], p_oth[...])
        ).astype(BF16)
        proj = slice(3 * half, 3 * half + width)
        own_w[proj, :] = t_dot(mixed_ref[:, cols], middle_b[:, :half]).astype(own_w.dtype)
        oth_w[proj, :] = t_dot(mixed_ref[:, cols], middle_b[:, half:]).astype(oth_w.dtype)

        def window(w, carry):
            rows = pl.ds(pl.multiple_of(w * PAD, PAD), PAD)
            keys, values = k_ref[rows, cols], v_ref[rows, cols]
            q_stack = stack_heads(q_ref[rows, cols], mask)
            g_stack = stack_heads(mg_ref[rows, cols], mask)
            probs = softmax(dot_t(q_stack, keys) + bias[b])
            pgrad = dot_t(g_stack, values)
            sgrad = probs * (pgrad - jnp.sum(probs * pgrad, axis=-1, keepdims=True))
            bgrad_ref[b] += sgrad
            score_b = sgrad.astype(BF16)
            q_grad = fold_heads(dot(score_b, keys), mask) * scale
            k_grad = t_dot(score_b, q_stack)
            v_grad = t_dot(probs.astype(BF16), g_stack)
            qvsum_ref[0:1, cols] += jnp.sum(q_grad, axis=0, keepdims=True)
            qvsum_ref[1:2, cols] += jnp.sum(v_grad, axis=0, keepdims=True)
            lin_ref[rows, 0:width] = q_grad.astype(BF16)
            lin_ref[rows, width:2 * width] = k_grad.astype(BF16)
            lin_ref[rows, 2 * width:3 * width] = v_grad.astype(BF16)
            return carry

        lax.fori_loop(0, 4, window, 0)
        lin = lin_ref[...]
        for s in range(3):
            part = lin[:, s * width:(s + 1) * width]
            here = slice(s * half, (s + 1) * half)
            own_w[here, :] = t_dot(ln[:, :half], part).astype(own_w.dtype)
            oth_w[here, :] = t_dot(ln[:, half:], part).astype(oth_w.dtype)
        first[0] = first[0] + dot_t(lin, w_own[...])
        first[1] = first[1] + dot_t(lin, w_oth[...])
    first_grad = jnp.concatenate(first, axis=1)
    rsum_ref[...] = jnp.zeros_like(rsum_ref)
    rsum_ref[0:1] = jnp.sum(first_grad * normed, axis=0, keepdims=True)
    rsum_ref[1:2] = jnp.sum(first_grad, axis=0, keepdims=True)
    in_grad = mgrad + norm_backward(first_grad, rvec[0:1], normed, inverse)
    in_ref[...] = t_dot(perm[...], in_grad.astype(BF16)).astype(BF16)


def total_kernel(n, g_ref, s_ref, out_ref, sum_ref, held, small, s1, r1, s2, r2, s3, r3):
    me = lax.axis_index("dp")
    chunk = g_ref.shape[0] // n

    def rows(index):
        return pl.ds(pl.multiple_of(index * chunk, chunk), chunk)

    barrier = pltpu.get_barrier_semaphore()
    for k in range(1, n):
        pl.semaphore_signal(
            barrier, inc=1, device_id={"dp": lax.rem(me + k, n)}, device_id_type=MESH
        )
    pl.semaphore_wait(barrier, n - 1)
    copies = []
    for k in range(1, n):
        peer = {"dp": lax.rem(me + k, n)}
        copies.append(
            pltpu.make_async_remote_copy(
                g_ref.at[rows(peer["dp"])], held.at[k], s1.at[k], r1.at[k], peer, MESH
            )
        )
        copies[-1].start()
    smalls = []
    for k in range(1, n):
        peer = {"dp": lax.rem(me + k, n)}
        smalls.append(
            pltpu.make_async_remote_copy(s_ref, small.at[me], s3.at[k], r3.at[k], peer, MESH)
        )
        smalls[-1].start()
    small[me] = s_ref[...]
    total = g_ref[rows(me)].astype(F32)
    for k in range(1, n):
        copies[k - 1].wait_recv()
        total = total + held[k].astype(F32)
    out_ref[rows(me)] = total.astype(BF16)
    gathers = []
    for k in range(1, n):
        peer = {"dp": lax.rem(me + k, n)}
        gathers.append(
            pltpu.make_async_remote_copy(
                out_ref.at[rows(me)], out_ref.at[rows(me)], s2.at[k], r2.at[k], peer, MESH
            )
        )
        gathers[-1].start()
    for copy in smalls:
        copy.wait()
    acc = small[0]
    for index in range(1, n):
        acc = acc + small[index]
    sum_ref[...] = acc
    for k in range(1, n):
        copies[k - 1].wait_send()
        gathers[k - 1].wait()


def dp_total(n, grads, small):
    chunk = grads.shape[0] // n
    dma = pltpu.SemaphoreType.DMA((n,))
    return pl.pallas_call(
        functools.partial(total_kernel, n),
        name="dp_total",
        out_shape=(
            jax.ShapeDtypeStruct(grads.shape, BF16),
            jax.ShapeDtypeStruct(small.shape, F32),
        ),
        in_specs=[VMEM] * 2,
        out_specs=(VMEM, VMEM),
        scratch_shapes=[
            pltpu.VMEM((n, chunk, grads.shape[1]), BF16),
            pltpu.VMEM((n,) + small.shape, F32),
        ]
        + [dma] * 6,
        compiler_params=pltpu.CompilerParams(
            collective_id=0, has_side_effects=True, vmem_limit_bytes=LIMIT
        ),
    )(grads, small)


def local_call(kernel, shapes, scratch, flops, *args):
    return pl.pallas_call(
        kernel,
        out_shape=tuple(jax.ShapeDtypeStruct(shape, dtype) for shape, dtype in shapes),
        in_specs=[VMEM] * len(args),
        out_specs=tuple([VMEM] * len(shapes)),
        scratch_shapes=[pltpu.VMEM(shape, dtype) for shape, dtype in scratch],
        compiler_params=pltpu.CompilerParams(vmem_limit_bytes=LIMIT),
        cost_estimate=pl.CostEstimate(flops=flops, bytes_accessed=1 << 23, transcendentals=0),
    )(*args)


def swap(value, axis):
    n = lax.axis_size(axis)
    return lax.ppermute(value, axis, [(i, n - 1 - i) for i in range(n)])


def quads(weight):
    over_row = swap(weight, "row")
    return weight, over_row, swap(weight, "col"), swap(over_row, "col")


def per_device(
    block_input, out_grad, first_gain, first_shift, qkv_weight, query_bias, value_bias,
    position_table, position_index, proj_weight, proj_bias, second_gain, second_shift,
    expand_weight, expand_bias, reduce_weight, reduce_bias,
):
    n = lax.axis_size("dp")
    row, col = lax.axis_index("row"), lax.axis_index("col")
    cores = lax.axis_size("col")
    half = block_input.shape[1]
    width = qkv_weight.shape[2]
    hid = expand_weight.shape[1]
    heads = position_table.shape[1]
    entries = position_table.shape[0]
    images = block_input.shape[0] // IMAGE
    mine = row * cores + col
    theirs = (1 - row) * cores + col

    def image_of(tokens):
        shaped = tokens.reshape(images, IMAGE, half)
        own = lax.dynamic_index_in_dim(shaped, mine, 0, keepdims=False)
        away = lax.dynamic_index_in_dim(shaped, theirs, 0, keepdims=False)
        return own, swap(away, "row")

    x_own, x_oth = image_of(block_input)
    rows_own = jnp.stack(
        [first_gain, first_shift, proj_bias, second_gain, second_shift, reduce_bias]
        + [jnp.zeros_like(first_gain)] * 2
    )
    rvec = jnp.concatenate([rows_own, swap(rows_own, "row")], axis=1)
    cols_own = jnp.concatenate(
        [query_bias, value_bias, expand_bias, position_table.reshape(-1)]
    )
    cols_oth = swap(cols_own, "col")
    qb = jnp.concatenate([query_bias, cols_oth[:width]])[None]
    vb = jnp.concatenate([value_bias, cols_oth[width:2 * width]])[None]
    eb = jnp.concatenate([expand_bias, cols_oth[2 * width:2 * width + hid]])[None]
    table_oth = cols_oth[2 * width + hid:].reshape(entries, heads)
    table = jnp.concatenate([position_table, table_oth], axis=1)
    qkv = quads(qkv_weight.reshape(half, 3 * width))
    proj = quads(proj_weight)
    g_own, g_oth = image_of(out_grad)
    expand = quads(expand_weight)
    reduce = quads(reduce_weight)
    proj = (proj[0], proj[1], proj[2], proj[3])

    one_hot = (
        position_index.reshape(-1)[:, None] == jnp.arange(entries, dtype=jnp.int32)[None, :]
    ).astype(F32)
    bias = lax.dot_general(
        table, one_hot, (((0,), (1,)), ((), ())), precision=lax.Precision.HIGHEST
    ).reshape(2, heads, WINDOW, WINDOW)
    bias = jnp.pad(bias, ((0, 0), (0, 0), (0, PAD - WINDOW), (0, 0)))
    bias = jnp.pad(
        bias, ((0, 0), (0, 0), (0, 0), (0, PAD - WINDOW)), constant_values=-1e30
    ).reshape(2, heads * PAD, PAD)

    perm = jnp.asarray(permutation(), BF16)
    full, full_h, full_e = 2 * half, 2 * width, 2 * hid
    queries, keys, values, mixed, middle, x_rows = local_call(
        attend_kernel,
        [((ROWS, full_h), BF16)] * 4 + [((ROWS, full), F32), ((ROWS, full), BF16)],
        [],
        2 * ROWS * full * full_h * 6,
        perm, x_own, x_oth, rvec, qb, vb, bias, *qkv, *proj,
    )
    mlp_rows = hid // half * half + hid
    block, mgrad, m_o, m_x, m_y, m_z, m_rsum, eb_grad = local_call(
        mlp_kernel,
        [((IMAGE, full), BF16), ((ROWS, full), F32)]
        + [((mlp_rows, half), F32)] * 2
        + [((mlp_rows, half), BF16)] * 2
        + [((8, full), F32), ((1, full_e), F32)],
        [((ROWS, full_e), F32), ((ROWS, full_e), BF16), ((ROWS, full_e), BF16)],
        2 * ROWS * full * full_e * 6,
        perm, g_own, g_oth, rvec, eb, middle, *expand, *reduce,
    )

    def spread(rows):
        own, away = rows[:, :half], rows[:, half:]
        beside = swap(own, "col")
        across = swap(away, "row")
        corner = swap(across, "col")
        pair = jnp.where(col == 0, jnp.stack([own, beside]), jnp.stack([beside, own]))
        other = jnp.where(col == 0, jnp.stack([across, corner]), jnp.stack([corner, across]))
        both = jnp.where(row == 0, jnp.stack([pair, other]), jnp.stack([other, pair]))
        return both.reshape(images * IMAGE, half)

    def scatter(own, over_row, over_col, over_both):
        own = own + swap(over_col, "col").astype(F32)
        over_row = over_row + swap(over_both, "col").astype(F32)
        return (own + swap(over_row.astype(BF16), "row").astype(F32)).astype(BF16)

    block_output = spread(block)
    mlp_part = scatter(m_o, m_x, m_y, m_z)
    att_rows = 3 * half + width
    in_rows, a_o, a_x, a_y, a_z, a_rsum, qv_grad, bgrad = local_call(
        back_kernel,
        [((IMAGE, full), BF16)]
        + [((att_rows, half), F32)] * 2
        + [((att_rows, half), BF16)] * 2
        + [((8, full), F32), ((8, full_h), F32), ((2, heads * PAD, PAD), F32)],
        [((ROWS, full_h), BF16), ((ROWS, 3 * width), BF16)],
        2 * ROWS * full * full_h * 12,
        perm, x_rows, queries, keys, values, mixed, mgrad, rvec, bias, *qkv, *proj,
    )
    input_grad = spread(in_rows).astype(F32)
    att_part = scatter(a_o, a_x, a_y, a_z)

    pairs = bgrad.reshape(2 * heads, PAD, PAD)[:, :WINDOW, :WINDOW].reshape(2 * heads, -1)
    table_grad = lax.dot_general(
        one_hot, pairs, (((0,), (1,)), ((), ())), precision=lax.Precision.HIGHEST
    )
    row_sums = jnp.concatenate([a_rsum[0:2], m_rsum[0:4]])
    row_o, row_x = row_sums[:, :half].reshape(-1), row_sums[:, half:].reshape(-1)

    def col_pack(b):
        return jnp.concatenate(
            [
                qv_grad[0, b * width:(b + 1) * width],
                qv_grad[1, b * width:(b + 1) * width],
                eb_grad[0, b * hid:(b + 1) * hid],
                table_grad[:, b * heads:(b + 1) * heads].reshape(-1),
            ]
        )

    size = row_o.shape[0]
    beside = swap(jnp.concatenate([row_o, row_x, col_pack(1)]), "col")
    row_o = row_o + beside[:size]
    row_x = row_x + beside[size:2 * size]
    col_o = col_pack(0) + beside[2 * size:]
    across = swap(jnp.concatenate([row_x, col_o]), "row")
    small = jnp.concatenate([row_o + across[:size], col_o + across[size:]])
    count = small.shape[0]
    lanes = -(-count // 1024) * 8
    small = jnp.pad(small, (0, lanes * 128 - count)).reshape(lanes, 128)

    grads, sums = dp_total(n, jnp.concatenate([mlp_part, att_part]), small)
    grads = grads.astype(F32)
    sums = sums.reshape(-1)
    expand_g = (
        grads[:hid].reshape(hid // half, half, half).transpose(1, 0, 2).reshape(half, hid)
    )
    reduce_g = grads[hid:2 * hid]
    qkv_g = grads[2 * hid:2 * hid + 3 * half].reshape(3, half, width).transpose(1, 0, 2)
    proj_g = grads[2 * hid + 3 * half:]
    first_gain_g, first_shift_g, proj_b_g, second_gain_g, second_shift_g, reduce_b_g = (
        sums[i * half:(i + 1) * half] for i in range(6)
    )
    rest = sums[size:]
    return (
        block_output,
        input_grad,
        first_gain_g,
        first_shift_g,
        qkv_g,
        rest[:width],
        rest[width:2 * width],
        rest[2 * width + hid:2 * width + hid + entries * heads].reshape(entries, heads),
        proj_g,
        proj_b_g,
        second_gain_g,
        second_shift_g,
        expand_g,
        rest[2 * width:2 * width + hid],
        reduce_g,
        reduce_b_g,
    )


def solution(mesh):
    in_specs = (
        P("dp", "row"), P("dp", "row"), P("row"), P("row"), P("row", None, "col"), P("col"),
        P("col"), P(None, "col"), P(), P("col", "row"), P("row"), P("row"), P("row"),
        P("row", "col"), P("col"), P("col", "row"), P("row"),
    )
    out_specs = (
        P("dp", "row"), P("dp", "row"), P("row"), P("row"), P("row", None, "col"), P("col"),
        P("col"), P(None, "col"), P("col", "row"), P("row"), P("row"), P("row"),
        P("row", "col"), P("col"), P("col", "row"), P("row"),
    )
    return jax.shard_map(
        per_device, mesh=mesh, in_specs=in_specs, out_specs=out_specs, check_vma=False
    )
```

```python
import functools

import jax
import jax.numpy as jnp
import numpy as np
from jax import lax
from jax.experimental import pallas as pl
from jax.experimental.pallas import tpu as pltpu
from jax.sharding import PartitionSpec as P

EPSILON = 1e-05
ROOT_HALF = 0.7071067811865476
GAUSS_PEAK = 0.3989422804014327
SIDE = 7
WINDOW = SIDE * SIDE
IMAGE = 4 * WINDOW
PAD = 64
ROWS = 4 * PAD
F32 = jnp.float32
BF16 = jnp.bfloat16
VMEM = pl.BlockSpec(memory_space=pltpu.VMEM)
MESH = pl.DeviceIdType.MESH
LIMIT = 60 * 1024 * 1024


def permutation():
    table = np.zeros((ROWS, IMAGE), np.float32)
    for window in range(4):
        for i in range(WINDOW):
            row = window // 2 * SIDE + i // SIDE
            column = window % 2 * SIDE + i % SIDE
            table[window * PAD + i, row * 2 * SIDE + column] = 1.0
    return table


def dot(left, right):
    return jnp.dot(left, right, preferred_element_type=F32)


def dot_t(left, right):
    return lax.dot_general(left, right, (((1,), (1,)), ((), ())), preferred_element_type=F32)


def t_dot(left, right):
    return lax.dot_general(left, right, (((0,), (0,)), ((), ())), preferred_element_type=F32)


def norm(values):
    center = jnp.mean(values, axis=-1, keepdims=True)
    shifted = values - center
    spread = jnp.mean(shifted * shifted, axis=-1, keepdims=True)
    inverse = lax.rsqrt(spread + EPSILON)
    return shifted * inverse, inverse


def norm_backward(upstream, gain, normed, inverse):
    scaled = upstream * gain
    return inverse * (
        scaled
        - jnp.mean(scaled, axis=-1, keepdims=True)
        - normed * jnp.mean(scaled * normed, axis=-1, keepdims=True)
    )


def head_mask(heads, width):
    size = width // heads
    head = lax.broadcasted_iota(jnp.int32, (heads, 1, width), 0)
    lane = lax.broadcasted_iota(jnp.int32, (heads, 1, width), 2)
    return (lane >= head * size) & (lane < (head + 1) * size)


def stack_heads(rows, mask):
    heads = mask.shape[0]
    wide = jnp.where(mask, rows.astype(F32)[None], 0.0)
    return wide.reshape(heads * rows.shape[0], rows.shape[1]).astype(BF16)


def fold_heads(stacked, mask):
    heads = mask.shape[0]
    split = stacked.reshape(heads, stacked.shape[0] // heads, stacked.shape[1])
    return jnp.sum(jnp.where(mask, split, 0.0), axis=0)


def softmax(scores):
    top = jnp.max(scores, axis=-1, keepdims=True)
    total = top + jnp.log(jnp.sum(jnp.exp(scores - top), axis=-1, keepdims=True))
    return jnp.exp(scores - total)


def attend_kernel(
    perm, x_own, x_oth, rvec, qb, vb, bias, w_oo, w_xo, w_ox, w_xx, p_oo, p_xo, p_ox, p_xx,
    q_out, k_out, v_out, mixed_out, middle_out, x_out,
):
    half = x_own.shape[1]
    width = p_oo.shape[0]
    heads = bias.shape[1] // PAD
    size = width // heads
    scale = size ** (-0.5)
    x = dot(perm[...], jnp.concatenate([x_own[...], x_oth[...]], axis=1))
    x_out[...] = x.astype(BF16)
    normed, _ = norm(x)
    ln = (normed * rvec[0:1] + rvec[1:2]).astype(BF16)
    mask = head_mask(heads, width)
    for b, (w_own, w_oth) in enumerate(((w_oo, w_xo), (w_ox, w_xx))):
        cols = slice(b * width, (b + 1) * width)
        for s, out in enumerate((q_out, k_out, v_out)):
            part = slice(s * width, (s + 1) * width)
            linear = dot(ln[:, :half], w_own[:, part]) + dot(ln[:, half:], w_oth[:, part])
            if s == 0:
                linear = (linear + qb[:, cols]) * scale
            if s == 2:
                linear = linear + vb[:, cols]
            out[:, cols] = linear.astype(BF16)

        def window(w, carry):
            rows = pl.ds(pl.multiple_of(w * PAD, PAD), PAD)
            scores = dot_t(stack_heads(q_out[rows, cols], mask), k_out[rows, cols]) + bias[b]
            probs = softmax(scores).astype(BF16)
            mixed_out[rows, cols] = fold_heads(dot(probs, v_out[rows, cols]), mask).astype(BF16)
            return carry

        lax.fori_loop(0, 4, window, 0)
    for a, (p_own, p_oth) in enumerate(((p_oo, p_ox), (p_xo, p_xx))):
        cols = slice(a * half, (a + 1) * half)
        middle_out[:, cols] = (
            x[:, cols]
            + (dot(mixed_out[:, :width], p_own[...]) + dot(mixed_out[:, width:], p_oth[...]))
            + rvec[2:3, cols]
        )


def mlp_kernel(
    perm, g_own, g_oth, rvec, eb, middle_ref, e_oo, e_xo, e_ox, e_xx, r_oo, r_xo, r_ox, r_xx,
    out_ref, away_ref, mgrad_ref, o_ref, x_ref, y_ref, z_ref, rsum_ref, ebg_ref,
    pre_ref, hidden_ref, pg_ref,
):
    half = g_own.shape[1]
    hid = e_oo.shape[1]
    middle = middle_ref[...]
    normed, inverse = norm(middle)
    ln = (normed * rvec[3:4] + rvec[4:5]).astype(BF16)
    grad = dot(perm[...], jnp.concatenate([g_own[...], g_oth[...]], axis=1))
    grad_b = grad.astype(BF16)
    for b, (e_own, e_oth, r_own, r_oth, own_w, oth_w) in enumerate(
        ((e_oo, e_xo, r_oo, r_xo, o_ref, x_ref), (e_ox, e_xx, r_ox, r_xx, y_ref, z_ref))
    ):
        for q in range(hid // half):
            here = slice(q * half, (q + 1) * half)
            cols = slice(b * hid + q * half, b * hid + (q + 1) * half)
            pre = dot(ln[:, :half], e_own[:, here]) + dot(ln[:, half:], e_oth[:, here])
            pre = pre + eb[:, cols]
            erf_half = 0.5 * (1.0 + lax.erf(pre * ROOT_HALF))
            hidden = (pre * erf_half).astype(BF16)
            hidden_ref[:, cols] = hidden
            slope = erf_half + pre * GAUSS_PEAK * jnp.exp(-0.5 * pre * pre)
            hgrad = dot_t(grad_b[:, :half], r_own[here, :]) + dot_t(grad_b[:, half:], r_oth[here, :])
            pgrad = (hgrad * slope).astype(BF16)
            pg_ref[:, cols] = pgrad
            ebg_ref[:, cols] = jnp.sum(pgrad.astype(F32), axis=0, keepdims=True)
            own_w[here, :] = t_dot(ln[:, :half], pgrad).astype(own_w.dtype)
            oth_w[here, :] = t_dot(ln[:, half:], pgrad).astype(oth_w.dtype)
            down = slice(hid + q * half, hid + (q + 1) * half)
            own_w[down, :] = t_dot(hidden, grad_b[:, :half]).astype(own_w.dtype)
            oth_w[down, :] = t_dot(hidden, grad_b[:, half:]).astype(oth_w.dtype)
    parts, grads = [], []
    for r_a, r_b, e_a, e_b in ((r_oo, r_ox, e_oo, e_ox), (r_xo, r_xx, e_xo, e_xx)):
        parts.append(dot(hidden_ref[:, :hid], r_a[...]) + dot(hidden_ref[:, hid:], r_b[...]))
        grads.append(dot_t(pg_ref[:, :hid], e_a[...]) + dot_t(pg_ref[:, hid:], e_b[...]))
    block = (middle + jnp.concatenate(parts, axis=1) + rvec[5:6]).astype(BF16)
    tokens = t_dot(perm[...], block).astype(BF16)
    out_ref[...] = tokens[:, :half]
    away_ref[...] = tokens[:, half:]
    second = jnp.concatenate(grads, axis=1)
    mgrad = grad + norm_backward(second, rvec[3:4], normed, inverse)
    mgrad_ref[...] = mgrad
    rsum_ref[...] = jnp.zeros_like(rsum_ref)
    rsum_ref[0:1] = jnp.sum(mgrad, axis=0, keepdims=True)
    rsum_ref[1:2] = jnp.sum(second * normed, axis=0, keepdims=True)
    rsum_ref[2:3] = jnp.sum(second, axis=0, keepdims=True)
    rsum_ref[3:4] = jnp.sum(grad, axis=0, keepdims=True)


def back_kernel(
    perm, x_ref, q_ref, k_ref, v_ref, mixed_ref, mgrad_ref, rvec, bias,
    w_oo, w_xo, w_ox, w_xx, p_oo, p_xo, p_ox, p_xx,
    in_ref, away_ref, o_ref, xx_ref, y_ref, z_ref, rsum_ref, qvsum_ref, bgrad_ref,
    mg_ref, lin_ref,
):
    width = p_oo.shape[0]
    half = p_oo.shape[1]
    heads = bias.shape[1] // PAD
    scale = (width // heads) ** (-0.5)
    normed, inverse = norm(x_ref[...].astype(F32))
    ln = (normed * rvec[0:1] + rvec[1:2]).astype(BF16)
    mgrad = mgrad_ref[...]
    middle_b = mgrad.astype(BF16)
    mask = head_mask(heads, width)
    bgrad_ref[...] = jnp.zeros_like(bgrad_ref)
    qvsum_ref[...] = jnp.zeros_like(qvsum_ref)
    first = [jnp.zeros((ROWS, half), F32), jnp.zeros((ROWS, half), F32)]
    for b, (p_own, p_oth, w_own, w_oth, own_w, oth_w) in enumerate(
        ((p_oo, p_xo, w_oo, w_xo, o_ref, xx_ref), (p_ox, p_xx, w_ox, w_xx, y_ref, z_ref))
    ):
        cols = slice(b * width, (b + 1) * width)
        mg_ref[:, cols] = (
            dot_t(middle_b[:, :half], p_own[...]) + dot_t(middle_b[:, half:], p_oth[...])
        ).astype(BF16)
        proj = slice(3 * half, 3 * half + width)
        own_w[proj, :] = t_dot(mixed_ref[:, cols], middle_b[:, :half]).astype(own_w.dtype)
        oth_w[proj, :] = t_dot(mixed_ref[:, cols], middle_b[:, half:]).astype(oth_w.dtype)

        def window(w, carry):
            rows = pl.ds(pl.multiple_of(w * PAD, PAD), PAD)
            keys, values = k_ref[rows, cols], v_ref[rows, cols]
            q_stack = stack_heads(q_ref[rows, cols], mask)
            g_stack = stack_heads(mg_ref[rows, cols], mask)
            probs = softmax(dot_t(q_stack, keys) + bias[b])
            pgrad = dot_t(g_stack, values)
            sgrad = probs * (pgrad - jnp.sum(probs * pgrad, axis=-1, keepdims=True))
            bgrad_ref[b] += sgrad
            score_b = sgrad.astype(BF16)
            q_grad = fold_heads(dot(score_b, keys), mask) * scale
            k_grad = t_dot(score_b, q_stack)
            v_grad = t_dot(probs.astype(BF16), g_stack)
            qvsum_ref[0:1, cols] += jnp.sum(q_grad, axis=0, keepdims=True)
            qvsum_ref[1:2, cols] += jnp.sum(v_grad, axis=0, keepdims=True)
            lin_ref[rows, 0:width] = q_grad.astype(BF16)
            lin_ref[rows, width:2 * width] = k_grad.astype(BF16)
            lin_ref[rows, 2 * width:3 * width] = v_grad.astype(BF16)
            return carry

        lax.fori_loop(0, 4, window, 0)
        lin = lin_ref[...]
        for s in range(3):
            part = lin[:, s * width:(s + 1) * width]
            here = slice(s * half, (s + 1) * half)
            own_w[here, :] = t_dot(ln[:, :half], part).astype(own_w.dtype)
            oth_w[here, :] = t_dot(ln[:, half:], part).astype(oth_w.dtype)
        first[0] = first[0] + dot_t(lin, w_own[...])
        first[1] = first[1] + dot_t(lin, w_oth[...])
    first_grad = jnp.concatenate(first, axis=1)
    rsum_ref[...] = jnp.zeros_like(rsum_ref)
    rsum_ref[0:1] = jnp.sum(first_grad * normed, axis=0, keepdims=True)
    rsum_ref[1:2] = jnp.sum(first_grad, axis=0, keepdims=True)
    in_grad = mgrad + norm_backward(first_grad, rvec[0:1], normed, inverse)
    tokens = t_dot(perm[...], in_grad.astype(BF16)).astype(BF16)
    in_ref[...] = tokens[:, :half]
    away_ref[...] = tokens[:, half:]


def total_kernel(
    n, size, srow, scol,
    mo, mx, my, mz, ao, ax, ay, az, s_ref, blk_own, blk_away, in_own, in_away,
    out_ref, sum_ref, blk_out, in_out,
    yr, zr, xb, xr, sb, sf, pr, tb, tf, qr, s_col, s_mid, s_row, s_dp,
    sem_c, sem_r, sem_p, sem_z, sem_gz, sem_gp, sem_s, sem_d, sem_o,
):
    me = lax.axis_index("dp")
    row, col = lax.axis_index("row"), lax.axis_index("col")
    cores = lax.axis_size("col")
    parity, place = lax.rem(me, 2), me // 2
    peers = n // 2
    over_col, over_row = {"col": 1 - col}, {"row": 1 - row}
    pair = {"dp": me + 1 - 2 * parity}
    block = size // n
    wide = size // 2
    chunks = out_ref.shape[0] // size
    mlp = mo.shape[0] // size

    def remote(src, dst, sems, index, device):
        return pltpu.make_async_remote_copy(
            src, dst, sems.at[(0,) + index], sems.at[(1,) + index], device, MESH
        )

    barrier = pltpu.get_barrier_semaphore()
    for device in [over_col, over_row] + [{"dp": lax.rem(me + k, n)} for k in range(1, n)]:
        pl.semaphore_signal(barrier, inc=1, device_id=device, device_id_type=MESH)
    pl.semaphore_wait(barrier, n + 1)

    def source(c, first, second):
        ref, at = (first, c) if c < mlp else (second, c - mlp)
        return ref.at[at * size:(at + 1) * size]

    live = {}

    def start(key, copy):
        live[key] = copy
        copy.start()

    def rows_of(c):
        return slice(c * size, (c + 1) * size)

    def begin(c):
        start(("y", c), remote(source(c, my, ay), yr.at[rows_of(c)], sem_c, (0, c), over_col))
        start(("z", c), remote(source(c, mz, az), zr.at[rows_of(c)], sem_c, (1, c), over_col))

    def stage_row(c):
        live["z", c].wait_recv()
        rows = rows_of(c)
        xb[rows] = (source(c, mx, ax)[...] + zr[rows].astype(F32)).astype(BF16)
        start(("r", c), remote(xb.at[rows], xr.at[rows], sem_r, (c,), over_row))

    def stage_pair(c):
        live["y", c].wait_recv()
        live["r", c].wait_recv()
        rows = rows_of(c)
        sf[...] = source(c, mo, ao)[...] + yr[rows].astype(F32) + xr[rows].astype(F32)
        sb[rows] = sf[...].astype(BF16)
        tf[c] = sf[pl.ds(pl.multiple_of(parity * wide, wide), wide)]
        away = pl.ds(pl.multiple_of(c * size + (1 - parity) * wide, wide), wide)
        start(("p", c), remote(sb.at[away], pr.at[c], sem_p, (c,), pair))

    def stage_rest(c):
        live["p", c].wait_recv()
        tf[c] = tf[c] + pr[c].astype(F32)
        tb[c] = tf[c].astype(BF16)
        for k in range(1, peers):
            there = lax.rem(place + k, peers)
            piece = pl.ds(pl.multiple_of(there * block, block), block)
            start(
                ("q", c, k),
                remote(
                    tb.at[c, piece], qr.at[c, k], sem_z, (c, k), {"dp": 2 * there + parity}
                ),
            )

    def mine_of(c):
        at = c * size + parity * wide + place * block
        return pl.ds(pl.multiple_of(at, block), block)

    def stage_sum(c):
        total = tf[c, pl.ds(pl.multiple_of(place * block, block), block)]
        for k in range(1, peers):
            live["q", c, k].wait_recv()
            total = total + qr[c, k].astype(F32)
        out_ref[mine_of(c)] = total.astype(BF16)
        for k in range(1, peers):
            there = lax.rem(place + k, peers)
            start(
                ("g", c, k),
                remote(
                    out_ref.at[mine_of(c)], out_ref.at[mine_of(c)], sem_gz, (c, k),
                    {"dp": 2 * there + parity},
                ),
            )

    def stage_back(c):
        for k in range(1, peers):
            live["g", c, k].wait_recv()
        half = pl.ds(pl.multiple_of(c * size + parity * wide, wide), wide)
        start(("b", c), remote(out_ref.at[half], out_ref.at[half], sem_gp, (c,), pair))

    mine = row * cores + col
    theirs = (1 - row) * cores + col

    def begin_small():
        first = 2 * srow + scol
        start("s0", remote(s_ref.at[0:first], s_col, sem_s, (0,), over_col))

    def small_row():
        live["s0"].wait_recv()
        s_mid[0:srow] = s_ref[srow:2 * srow] + s_col[srow:2 * srow]
        s_mid[srow:srow + scol] = (
            s_ref[2 * srow + scol:2 * srow + 2 * scol] + s_col[2 * srow:2 * srow + scol]
        )
        start("s1", remote(s_mid, s_row, sem_s, (1,), over_row))

    def small_dp():
        live["s1"].wait_recv()
        s_dp[me, 0:srow] = s_ref[0:srow] + s_col[0:srow] + s_row[0:srow]
        s_dp[me, srow:srow + scol] = s_mid[srow:srow + scol] + s_row[srow:srow + scol]
        for k in range(1, n):
            peer = {"dp": lax.rem(me + k, n)}
            start(("s2", k), remote(s_dp.at[me], s_dp.at[me], sem_d, (k,), peer))

    def small_sum():
        for k in range(1, n):
            live["s2", k].wait_recv()
        acc = s_dp[0]
        for index in range(1, n):
            acc = acc + s_dp[index]
        sum_ref[...] = acc

    def begin_spread(i, own, away, out):
        start(("o0", i), remote(own, out.at[mine], sem_o, (i, 0), over_col))
        start(("o1", i), remote(away, out.at[mine], sem_o, (i, 1), over_row))
        out[mine] = own[...]

    def forward(i, out):
        live["o1", i].wait_recv()
        start(("o2", i), remote(out.at[theirs], out.at[theirs], sem_o, (i, 2), over_col))

    for c in range(chunks):
        begin(c)
    begin_small()
    stages = (stage_row, stage_pair, stage_rest, stage_sum, stage_back)
    for step in range(chunks + len(stages) - 1):
        for k in reversed(range(len(stages))):
            if 0 <= step - k < chunks:
                stages[k](step - k)
        if step == 0:
            small_row()
        if step == 1:
            small_dp()
        if step == 2:
            begin_spread(0, blk_own, blk_away, blk_out)
        if step == 3:
            begin_spread(1, in_own, in_away, in_out)
    forward(0, blk_out)
    forward(1, in_out)
    small_sum()
    for key, copy in live.items():
        copy.wait_send()
        if key[0] in ("b", "o0", "o2"):
            copy.wait_recv()


def group_total(n, mlp, att, small, srow, scol, block, rows_in, images):
    rows = mlp[0].shape[0] + att[0].shape[0]
    half = mlp[0].shape[1]
    size = max(n * 16, 512)
    chunks, peers, wide = rows // size, n // 2, size // 2
    dma = pltpu.SemaphoreType.DMA
    spread = jax.ShapeDtypeStruct((images,) + block[0].shape, BF16)
    args = (*mlp, *att, small, *block, *rows_in)
    return pl.pallas_call(
        functools.partial(total_kernel, n, size, srow, scol),
        name="group_total",
        out_shape=(
            jax.ShapeDtypeStruct((rows, half), BF16),
            jax.ShapeDtypeStruct((srow + scol, 128), F32),
            spread,
            spread,
        ),
        in_specs=[VMEM] * len(args),
        out_specs=(VMEM,) * 4,
        scratch_shapes=[pltpu.VMEM((rows, half), BF16)] * 4
        + [
            pltpu.VMEM((rows, half), BF16),
            pltpu.VMEM((size, half), F32),
            pltpu.VMEM((chunks, wide, half), BF16),
            pltpu.VMEM((chunks, wide, half), BF16),
            pltpu.VMEM((chunks, wide, half), F32),
            pltpu.VMEM((chunks, peers, size // n, half), BF16),
            pltpu.VMEM((2 * srow + scol, 128), F32),
            pltpu.VMEM((srow + scol, 128), F32),
            pltpu.VMEM((srow + scol, 128), F32),
            pltpu.VMEM((n, srow + scol, 128), F32),
            dma((2, 2, chunks)),
            dma((2, chunks)),
            dma((2, chunks)),
            dma((2, chunks, peers)),
            dma((2, chunks, peers)),
            dma((2, chunks)),
            dma((2, 2)),
            dma((2, n)),
            dma((2, 2, 3)),
        ],
        compiler_params=pltpu.CompilerParams(
            collective_id=0, has_side_effects=True, vmem_limit_bytes=LIMIT
        ),
    )(*args)


def local_call(kernel, shapes, scratch, flops, *args):
    return pl.pallas_call(
        kernel,
        out_shape=tuple(jax.ShapeDtypeStruct(shape, dtype) for shape, dtype in shapes),
        in_specs=[VMEM] * len(args),
        out_specs=tuple([VMEM] * len(shapes)),
        scratch_shapes=[pltpu.VMEM(shape, dtype) for shape, dtype in scratch],
        compiler_params=pltpu.CompilerParams(vmem_limit_bytes=LIMIT),
        cost_estimate=pl.CostEstimate(flops=flops, bytes_accessed=1 << 23, transcendentals=0),
    )(*args)


def swap(value, axis):
    n = lax.axis_size(axis)
    return lax.ppermute(value, axis, [(i, n - 1 - i) for i in range(n)])


def quads(weight):
    over_row = swap(weight, "row")
    return weight, over_row, swap(weight, "col"), swap(over_row, "col")


def per_device(
    block_input, out_grad, first_gain, first_shift, qkv_weight, query_bias, value_bias,
    position_table, position_index, proj_weight, proj_bias, second_gain, second_shift,
    expand_weight, expand_bias, reduce_weight, reduce_bias,
):
    n = lax.axis_size("dp")
    row, col = lax.axis_index("row"), lax.axis_index("col")
    cores = lax.axis_size("col")
    half = block_input.shape[1]
    width = qkv_weight.shape[2]
    hid = expand_weight.shape[1]
    heads = position_table.shape[1]
    entries = position_table.shape[0]
    images = block_input.shape[0] // IMAGE
    mine = row * cores + col
    theirs = (1 - row) * cores + col

    def image_of(tokens):
        shaped = tokens.reshape(images, IMAGE, half)
        own = lax.dynamic_index_in_dim(shaped, mine, 0, keepdims=False)
        away = lax.dynamic_index_in_dim(shaped, theirs, 0, keepdims=False)
        return own, swap(away, "row")

    x_own, x_oth = image_of(block_input)
    rows_own = jnp.stack(
        [first_gain, first_shift, proj_bias, second_gain, second_shift, reduce_bias]
        + [jnp.zeros_like(first_gain)] * 2
    )
    rvec = jnp.concatenate([rows_own, swap(rows_own, "row")], axis=1)
    cols_own = jnp.concatenate(
        [query_bias, value_bias, expand_bias, position_table.reshape(-1)]
    )
    cols_oth = swap(cols_own, "col")
    qb = jnp.concatenate([query_bias, cols_oth[:width]])[None]
    vb = jnp.concatenate([value_bias, cols_oth[width:2 * width]])[None]
    eb = jnp.concatenate([expand_bias, cols_oth[2 * width:2 * width + hid]])[None]
    table_oth = cols_oth[2 * width + hid:].reshape(entries, heads)
    table = jnp.concatenate([position_table, table_oth], axis=1)
    qkv = quads(qkv_weight.reshape(half, 3 * width))
    proj = quads(proj_weight)
    g_own, g_oth = image_of(out_grad)
    expand = quads(expand_weight)
    reduce = quads(reduce_weight)
    proj = (proj[0], proj[1], proj[2], proj[3])

    one_hot = (
        position_index.reshape(-1)[:, None] == jnp.arange(entries, dtype=jnp.int32)[None, :]
    ).astype(F32)
    bias = lax.dot_general(
        table, one_hot, (((0,), (1,)), ((), ())), precision=lax.Precision.HIGHEST
    ).reshape(2, heads, WINDOW, WINDOW)
    bias = jnp.pad(bias, ((0, 0), (0, 0), (0, PAD - WINDOW), (0, 0)))
    bias = jnp.pad(
        bias, ((0, 0), (0, 0), (0, 0), (0, PAD - WINDOW)), constant_values=-1e30
    ).reshape(2, heads * PAD, PAD)

    perm = jnp.asarray(permutation(), BF16)
    full, full_h, full_e = 2 * half, 2 * width, 2 * hid
    queries, keys, values, mixed, middle, x_rows = local_call(
        attend_kernel,
        [((ROWS, full_h), BF16)] * 4 + [((ROWS, full), F32), ((ROWS, full), BF16)],
        [],
        2 * ROWS * full * full_h * 6,
        perm, x_own, x_oth, rvec, qb, vb, bias, *qkv, *proj,
    )
    mlp_rows = hid // half * half + hid
    block, block_away, mgrad, m_o, m_x, m_y, m_z, m_rsum, eb_grad = local_call(
        mlp_kernel,
        [((IMAGE, half), BF16)] * 2 + [((ROWS, full), F32)]
        + [((mlp_rows, half), F32)] * 2
        + [((mlp_rows, half), BF16)] * 2
        + [((8, full), F32), ((1, full_e), F32)],
        [((ROWS, full_e), F32), ((ROWS, full_e), BF16), ((ROWS, full_e), BF16)],
        2 * ROWS * full * full_e * 6,
        perm, g_own, g_oth, rvec, eb, middle, *expand, *reduce,
    )

    att_rows = 3 * half + width
    in_rows, in_away, a_o, a_x, a_y, a_z, a_rsum, qv_grad, bgrad = local_call(
        back_kernel,
        [((IMAGE, half), BF16)] * 2
        + [((att_rows, half), F32)] * 2
        + [((att_rows, half), BF16)] * 2
        + [((8, full), F32), ((8, full_h), F32), ((2, heads * PAD, PAD), F32)],
        [((ROWS, full_h), BF16), ((ROWS, 3 * width), BF16)],
        2 * ROWS * full * full_h * 12,
        perm, x_rows, queries, keys, values, mixed, mgrad, rvec, bias, *qkv, *proj,
    )

    pairs = bgrad.reshape(2 * heads, PAD, PAD)[:, :WINDOW, :WINDOW].reshape(2 * heads, -1)
    table_grad = lax.dot_general(
        one_hot, pairs, (((0,), (1,)), ((), ())), precision=lax.Precision.HIGHEST
    )
    row_sums = jnp.concatenate([a_rsum[0:2], m_rsum[0:4]])
    row_o, row_x = row_sums[:, :half].reshape(-1), row_sums[:, half:].reshape(-1)

    def col_pack(b):
        return jnp.concatenate(
            [
                qv_grad[0, b * width:(b + 1) * width],
                qv_grad[1, b * width:(b + 1) * width],
                eb_grad[0, b * hid:(b + 1) * hid],
                table_grad[:, b * heads:(b + 1) * heads].reshape(-1),
            ]
        )

    size = row_o.shape[0]

    def lanes(vector):
        count = -(-vector.shape[0] // 1024) * 1024
        return jnp.pad(vector, (0, count - vector.shape[0])).reshape(-1, 128)

    row_o, row_x, col_o, col_x = lanes(row_o), lanes(row_x), lanes(col_pack(0)), lanes(col_pack(1))
    srow, scol = row_o.shape[0], col_o.shape[0]
    grads, sums, block_output, input_grad = group_total(
        n, (m_o, m_x, m_y, m_z), (a_o, a_x, a_y, a_z),
        jnp.concatenate([row_o, row_x, col_x, col_o]), srow, scol,
        (block, block_away), (in_rows, in_away), images,
    )
    block_output = block_output.reshape(images * IMAGE, half)
    input_grad = input_grad.astype(F32).reshape(images * IMAGE, half)
    grads = grads.astype(F32)
    sums = sums.reshape(-1)
    expand_g = (
        grads[:hid].reshape(hid // half, half, half).transpose(1, 0, 2).reshape(half, hid)
    )
    reduce_g = grads[hid:2 * hid]
    qkv_g = grads[2 * hid:2 * hid + 3 * half].reshape(3, half, width).transpose(1, 0, 2)
    proj_g = grads[2 * hid + 3 * half:]
    first_gain_g, first_shift_g, proj_b_g, second_gain_g, second_shift_g, reduce_b_g = (
        sums[i * half:(i + 1) * half] for i in range(6)
    )
    rest = sums[srow * 128:]
    return (
        block_output,
        input_grad,
        first_gain_g,
        first_shift_g,
        qkv_g,
        rest[:width],
        rest[width:2 * width],
        rest[2 * width + hid:2 * width + hid + entries * heads].reshape(entries, heads),
        proj_g,
        proj_b_g,
        second_gain_g,
        second_shift_g,
        expand_g,
        rest[2 * width:2 * width + hid],
        reduce_g,
        reduce_b_g,
    )


def solution(mesh):
    in_specs = (
        P("dp", "row"), P("dp", "row"), P("row"), P("row"), P("row", None, "col"), P("col"),
        P("col"), P(None, "col"), P(), P("col", "row"), P("row"), P("row"), P("row"),
        P("row", "col"), P("col"), P("col", "row"), P("row"),
    )
    out_specs = (
        P("dp", "row"), P("dp", "row"), P("row"), P("row"), P("row", None, "col"), P("col"),
        P("col"), P(None, "col"), P("col", "row"), P("row"), P("row"), P("row"),
        P("row", "col"), P("col"), P("col", "row"), P("row"),
    )
    return jax.shard_map(
        per_device, mesh=mesh, in_specs=in_specs, out_specs=out_specs, check_vma=False
    )
```

```python
import functools

import jax
import jax.numpy as jnp
import numpy as np
from jax import lax
from jax.experimental import pallas as pl
from jax.experimental.pallas import tpu as pltpu
from jax.sharding import PartitionSpec as P

EPSILON = 1e-05
ROOT_HALF = 0.7071067811865476
GAUSS_PEAK = 0.3989422804014327
SIDE = 7
WINDOW = SIDE * SIDE
IMAGE = 4 * WINDOW
PAD = 64
ROWS = 4 * PAD
F32 = jnp.float32
BF16 = jnp.bfloat16
VMEM = pl.BlockSpec(memory_space=pltpu.VMEM)
MESH = pl.DeviceIdType.MESH
LIMIT = 60 * 1024 * 1024

def permutation():
    table = np.zeros((ROWS, IMAGE), np.float32)
    for window in range(4):
        for i in range(WINDOW):
            row = window // 2 * SIDE + i // SIDE
            column = window % 2 * SIDE + i % SIDE
            table[window * PAD + i, row * 2 * SIDE + column] = 1.0
    return table


def dot(left, right):
    return jnp.dot(left, right, preferred_element_type=F32)


def dot_t(left, right):
    return lax.dot_general(left, right, (((1,), (1,)), ((), ())), preferred_element_type=F32)


def t_dot(left, right):
    return lax.dot_general(left, right, (((0,), (0,)), ((), ())), preferred_element_type=F32)


def norm(values):
    center = jnp.mean(values, axis=-1, keepdims=True)
    shifted = values - center
    spread = jnp.mean(shifted * shifted, axis=-1, keepdims=True)
    inverse = lax.rsqrt(spread + EPSILON)
    return shifted * inverse, inverse


def norm_backward(upstream, gain, normed, inverse):
    scaled = upstream * gain
    return inverse * (
        scaled
        - jnp.mean(scaled, axis=-1, keepdims=True)
        - normed * jnp.mean(scaled * normed, axis=-1, keepdims=True)
    )


def head_mask(heads, width):
    size = width // heads
    head = lax.broadcasted_iota(jnp.int32, (heads, 1, width), 0)
    lane = lax.broadcasted_iota(jnp.int32, (heads, 1, width), 2)
    return (lane >= head * size) & (lane < (head + 1) * size)


def stack_heads(rows, mask):
    heads = mask.shape[0]
    wide = jnp.where(mask, rows.astype(F32)[None], 0.0)
    return wide.reshape(heads * rows.shape[0], rows.shape[1]).astype(BF16)


def fold_heads(stacked, mask):
    heads = mask.shape[0]
    split = stacked.reshape(heads, stacked.shape[0] // heads, stacked.shape[1])
    return jnp.sum(jnp.where(mask, split, 0.0), axis=0)


def softmax(scores):
    top = jnp.max(scores, axis=-1, keepdims=True)
    total = top + jnp.log(jnp.sum(jnp.exp(scores - top), axis=-1, keepdims=True))
    return jnp.exp(scores - total)


def attend_kernel(
    perm, x_own, x_oth, rvec, qb, vb, bias, w_oo, w_xo, w_ox, w_xx, p_oo, p_xo, p_ox, p_xx,
    q_out, k_out, v_out, mixed_out, middle_out, x_out,
):
    half = x_own.shape[1]
    width = p_oo.shape[0]
    heads = bias.shape[1] // PAD
    size = width // heads
    scale = size ** (-0.5)
    x = dot(perm[...], jnp.concatenate([x_own[...], x_oth[...]], axis=1))
    x_out[...] = x.astype(BF16)
    normed, _ = norm(x)
    ln = (normed * rvec[0:1] + rvec[1:2]).astype(BF16)
    mask = head_mask(heads, width)
    for b, (w_own, w_oth) in enumerate(((w_oo, w_xo), (w_ox, w_xx))):
        cols = slice(b * width, (b + 1) * width)
        for s, out in enumerate((q_out, k_out, v_out)):
            part = slice(s * width, (s + 1) * width)
            linear = dot(ln[:, :half], w_own[:, part]) + dot(ln[:, half:], w_oth[:, part])
            if s == 0:
                linear = (linear + qb[:, cols]) * scale
            if s == 2:
                linear = linear + vb[:, cols]
            out[:, cols] = linear.astype(BF16)

        def window(w, carry):
            rows = pl.ds(pl.multiple_of(w * PAD, PAD), PAD)
            scores = dot_t(stack_heads(q_out[rows, cols], mask), k_out[rows, cols]) + bias[b]
            probs = softmax(scores).astype(BF16)
            mixed_out[rows, cols] = fold_heads(dot(probs, v_out[rows, cols]), mask).astype(BF16)
            return carry

        lax.fori_loop(0, 4, window, 0)
    for a, (p_own, p_oth) in enumerate(((p_oo, p_ox), (p_xo, p_xx))):
        cols = slice(a * half, (a + 1) * half)
        middle_out[:, cols] = (
            x[:, cols]
            + (dot(mixed_out[:, :width], p_own[...]) + dot(mixed_out[:, width:], p_oth[...]))
            + rvec[2:3, cols]
        )


def mlp_kernel(
    perm, g_own, g_oth, rvec, eb, middle_ref, e_oo, e_xo, e_ox, e_xx, r_oo, r_xo, r_ox, r_xx,
    out_ref, away_ref, mgrad_ref, o_ref, x_ref, y_ref, z_ref, rsum_ref, ebg_ref,
    pre_ref, hidden_ref, pg_ref,
):
    half = g_own.shape[1]
    hid = e_oo.shape[1]
    middle = middle_ref[...]
    normed, inverse = norm(middle)
    ln = (normed * rvec[3:4] + rvec[4:5]).astype(BF16)
    grad = dot(perm[...], jnp.concatenate([g_own[...], g_oth[...]], axis=1))
    grad_b = grad.astype(BF16)
    for b, (e_own, e_oth, r_own, r_oth, own_w, oth_w) in enumerate(
        ((e_oo, e_xo, r_oo, r_xo, o_ref, x_ref), (e_ox, e_xx, r_ox, r_xx, y_ref, z_ref))
    ):
        for q in range(hid // half):
            here = slice(q * half, (q + 1) * half)
            cols = slice(b * hid + q * half, b * hid + (q + 1) * half)
            pre = dot(ln[:, :half], e_own[:, here]) + dot(ln[:, half:], e_oth[:, here])
            pre = pre + eb[:, cols]
            erf_half = 0.5 * (1.0 + lax.erf(pre * ROOT_HALF))
            hidden = (pre * erf_half).astype(BF16)
            hidden_ref[:, cols] = hidden
            slope = erf_half + pre * GAUSS_PEAK * jnp.exp(-0.5 * pre * pre)
            hgrad = dot_t(grad_b[:, :half], r_own[here, :]) + dot_t(grad_b[:, half:], r_oth[here, :])
            pgrad = (hgrad * slope).astype(BF16)
            pg_ref[:, cols] = pgrad
            ebg_ref[:, cols] = jnp.sum(pgrad.astype(F32), axis=0, keepdims=True)
            own_w[here, :] = t_dot(ln[:, :half], pgrad).astype(own_w.dtype)
            oth_w[here, :] = t_dot(ln[:, half:], pgrad).astype(oth_w.dtype)
            down = slice(hid + q * half, hid + (q + 1) * half)
            own_w[down, :] = t_dot(hidden, grad_b[:, :half]).astype(own_w.dtype)
            oth_w[down, :] = t_dot(hidden, grad_b[:, half:]).astype(oth_w.dtype)
    parts, grads = [], []
    for r_a, r_b, e_a, e_b in ((r_oo, r_ox, e_oo, e_ox), (r_xo, r_xx, e_xo, e_xx)):
        parts.append(dot(hidden_ref[:, :hid], r_a[...]) + dot(hidden_ref[:, hid:], r_b[...]))
        grads.append(dot_t(pg_ref[:, :hid], e_a[...]) + dot_t(pg_ref[:, hid:], e_b[...]))
    block = (middle + jnp.concatenate(parts, axis=1) + rvec[5:6]).astype(BF16)
    tokens = t_dot(perm[...], block).astype(BF16)
    out_ref[...] = tokens[:, :half]
    away_ref[...] = tokens[:, half:]
    second = jnp.concatenate(grads, axis=1)
    mgrad = grad + norm_backward(second, rvec[3:4], normed, inverse)
    mgrad_ref[...] = mgrad
    rsum_ref[...] = jnp.zeros_like(rsum_ref)
    rsum_ref[0:1] = jnp.sum(mgrad, axis=0, keepdims=True)
    rsum_ref[1:2] = jnp.sum(second * normed, axis=0, keepdims=True)
    rsum_ref[2:3] = jnp.sum(second, axis=0, keepdims=True)
    rsum_ref[3:4] = jnp.sum(grad, axis=0, keepdims=True)


def back_kernel(
    perm, x_ref, q_ref, k_ref, v_ref, mixed_ref, mgrad_ref, rvec, bias,
    w_oo, w_xo, w_ox, w_xx, p_oo, p_xo, p_ox, p_xx,
    in_ref, away_ref, o_ref, xx_ref, y_ref, z_ref, rsum_ref, qvsum_ref, bgrad_ref,
    mg_ref, lin_ref,
):
    width = p_oo.shape[0]
    half = p_oo.shape[1]
    heads = bias.shape[1] // PAD
    scale = (width // heads) ** (-0.5)
    normed, inverse = norm(x_ref[...].astype(F32))
    ln = (normed * rvec[0:1] + rvec[1:2]).astype(BF16)
    mgrad = mgrad_ref[...]
    middle_b = mgrad.astype(BF16)
    mask = head_mask(heads, width)
    bgrad_ref[...] = jnp.zeros_like(bgrad_ref)
    qvsum_ref[...] = jnp.zeros_like(qvsum_ref)
    first = [jnp.zeros((ROWS, half), F32), jnp.zeros((ROWS, half), F32)]
    for b, (p_own, p_oth, w_own, w_oth, own_w, oth_w) in enumerate(
        ((p_oo, p_xo, w_oo, w_xo, o_ref, xx_ref), (p_ox, p_xx, w_ox, w_xx, y_ref, z_ref))
    ):
        cols = slice(b * width, (b + 1) * width)
        mg_ref[:, cols] = (
            dot_t(middle_b[:, :half], p_own[...]) + dot_t(middle_b[:, half:], p_oth[...])
        ).astype(BF16)
        proj = slice(3 * half, 3 * half + width)
        own_w[proj, :] = t_dot(mixed_ref[:, cols], middle_b[:, :half]).astype(own_w.dtype)
        oth_w[proj, :] = t_dot(mixed_ref[:, cols], middle_b[:, half:]).astype(oth_w.dtype)

        def window(w, carry):
            rows = pl.ds(pl.multiple_of(w * PAD, PAD), PAD)
            keys, values = k_ref[rows, cols], v_ref[rows, cols]
            q_stack = stack_heads(q_ref[rows, cols], mask)
            g_stack = stack_heads(mg_ref[rows, cols], mask)
            probs = softmax(dot_t(q_stack, keys) + bias[b])
            pgrad = dot_t(g_stack, values)
            sgrad = probs * (pgrad - jnp.sum(probs * pgrad, axis=-1, keepdims=True))
            bgrad_ref[b] += sgrad
            score_b = sgrad.astype(BF16)
            q_grad = fold_heads(dot(score_b, keys), mask) * scale
            k_grad = t_dot(score_b, q_stack)
            v_grad = t_dot(probs.astype(BF16), g_stack)
            qvsum_ref[0:1, cols] += jnp.sum(q_grad, axis=0, keepdims=True)
            qvsum_ref[1:2, cols] += jnp.sum(v_grad, axis=0, keepdims=True)
            lin_ref[rows, 0:width] = q_grad.astype(BF16)
            lin_ref[rows, width:2 * width] = k_grad.astype(BF16)
            lin_ref[rows, 2 * width:3 * width] = v_grad.astype(BF16)
            return carry

        lax.fori_loop(0, 4, window, 0)
        lin = lin_ref[...]
        for s in range(3):
            part = lin[:, s * width:(s + 1) * width]
            here = slice(s * half, (s + 1) * half)
            own_w[here, :] = t_dot(ln[:, :half], part).astype(own_w.dtype)
            oth_w[here, :] = t_dot(ln[:, half:], part).astype(oth_w.dtype)
        first[0] = first[0] + dot_t(lin, w_own[...])
        first[1] = first[1] + dot_t(lin, w_oth[...])
    first_grad = jnp.concatenate(first, axis=1)
    rsum_ref[...] = jnp.zeros_like(rsum_ref)
    rsum_ref[0:1] = jnp.sum(first_grad * normed, axis=0, keepdims=True)
    rsum_ref[1:2] = jnp.sum(first_grad, axis=0, keepdims=True)
    in_grad = mgrad + norm_backward(first_grad, rvec[0:1], normed, inverse)
    tokens = t_dot(perm[...], in_grad.astype(BF16)).astype(BF16)
    in_ref[...] = tokens[:, :half]
    away_ref[...] = tokens[:, half:]


def gather_kernel(
    n, x_ref, g_ref, rvec, cvec, qkv, proj, expand, reduce,
    x_out, g_out, r_out, c_out,
    q_r, q_c, q_b, p_r, p_c, p_b, e_r, e_c, e_b, d_r, d_c, d_b,
    sem_y, sem_x, sem_c, sem_f, sem_o,
):
    me = lax.axis_index("dp")
    parity = lax.rem(me, 2)
    over_col = {"col": 1 - lax.axis_index("col")}
    over_row = {"row": 1 - lax.axis_index("row")}
    pair = {"dp": me + 1 - 2 * parity}
    barrier = pltpu.get_barrier_semaphore()
    for device in (over_col, over_row, pair):
        pl.semaphore_signal(barrier, inc=1, device_id=device, device_id_type=MESH)
    pl.semaphore_wait(barrier, 3)

    def remote(src, dst, sems, index, device):
        copy = pltpu.make_async_remote_copy(
            src, dst, sems.at[0, index], sems.at[1, index], device, MESH
        )
        copy.start()
        return copy

    weights = ((qkv, q_r, q_c, q_b), (proj, p_r, p_c, p_b), (expand, e_r, e_c, e_b), (reduce, d_r, d_c, d_b))
    pieces = [(w, j) for w in range(4) for j in range(2)]

    def rows(w, j, side):
        depth = weights[w][0].shape[0] // 4
        return pl.ds(pl.multiple_of(side * 2 * depth + j * depth, depth), depth)

    done = [
        remote(x_ref, x_out, sem_o, 0, over_row),
        remote(rvec, r_out, sem_o, 1, over_row),
        remote(cvec, c_out, sem_o, 2, over_col),
    ]
    along = []
    for i, (w, j) in enumerate(pieces):
        if i == 4:
            done.append(remote(g_ref, g_out, sem_o, 3, over_row))
        here = rows(w, j, parity)
        along.append(remote(weights[w][0].at[here], weights[w][1].at[here], sem_y, i, over_row))
    for w in range(4):
        done.append(remote(weights[w][0], weights[w][2], sem_c, w, over_col))
    across = []
    for i in range(len(pieces) + 1):
        if i < len(pieces):
            w, j = pieces[i]
            here = rows(w, j, parity)
            along[i].wait_recv()
            across.append(remote(weights[w][1].at[here], weights[w][1].at[here], sem_x, i, pair))
            done.append(remote(weights[w][1].at[here], weights[w][3].at[here], sem_f, i, over_col))
        if i > 0:
            w, j = pieces[i - 1]
            there = rows(w, j, 1 - parity)
            across[i - 1].wait_recv()
            done.append(
                remote(
                    weights[w][1].at[there], weights[w][3].at[there], sem_f,
                    len(pieces) + i - 1, over_col,
                )
            )
    for copy in along + across:
        copy.wait_send()
    for copy in done:
        copy.wait()


def gather(n, x, g, rvec, cvec, *weights):
    dma = pltpu.SemaphoreType.DMA
    args = (x, g, rvec, cvec) + weights
    outs = args[:4] + tuple(weight for weight in weights for _ in range(3))
    got = pl.pallas_call(
        functools.partial(gather_kernel, n),
        name="group_gather",
        out_shape=tuple(jax.ShapeDtypeStruct(out.shape, out.dtype) for out in outs),
        in_specs=[VMEM] * len(args),
        out_specs=(VMEM,) * len(outs),
        scratch_shapes=[dma((2, 8)), dma((2, 8)), dma((2, 4)), dma((2, 16)), dma((2, 4))],
        compiler_params=pltpu.CompilerParams(
            collective_id=1, has_side_effects=True, vmem_limit_bytes=LIMIT
        ),
    )(*args)
    return got[:4], [(w,) + tuple(got[4 + 3 * i:7 + 3 * i]) for i, w in enumerate(weights)]


def total_kernel(
    n, size, srow, scol,
    mo, mx, my, mz, ao, ax, ay, az, s_ref, blk_own, blk_away, in_own, in_away,
    out_ref, sum_ref, blk_out, in_out,
    yr, zr, xb, xr, sb, sf, pr, tb, tf, qr, s_col, s_mid, s_row, s_dp,
    sem_c, sem_r, sem_p, sem_z, sem_gz, sem_gp, sem_s, sem_d, sem_o,
):
    me = lax.axis_index("dp")
    row, col = lax.axis_index("row"), lax.axis_index("col")
    cores = lax.axis_size("col")
    parity, place = lax.rem(me, 2), me // 2
    peers = n // 2
    over_col, over_row = {"col": 1 - col}, {"row": 1 - row}
    pair = {"dp": me + 1 - 2 * parity}
    block = size // n
    wide = size // 2
    chunks = out_ref.shape[0] // size
    mlp = mo.shape[0] // size

    def remote(src, dst, sems, index, device):
        return pltpu.make_async_remote_copy(
            src, dst, sems.at[(0,) + index], sems.at[(1,) + index], device, MESH
        )

    barrier = pltpu.get_barrier_semaphore()
    for device in [over_col, over_row] + [{"dp": lax.rem(me + k, n)} for k in range(1, n)]:
        pl.semaphore_signal(barrier, inc=1, device_id=device, device_id_type=MESH)
    pl.semaphore_wait(barrier, n + 1)

    def source(c, first, second):
        ref, at = (first, c) if c < mlp else (second, c - mlp)
        return ref.at[at * size:(at + 1) * size]

    live = {}

    def start(key, copy):
        live[key] = copy
        copy.start()

    def rows_of(c):
        return slice(c * size, (c + 1) * size)

    def begin(c):
        start(("y", c), remote(source(c, my, ay), yr.at[rows_of(c)], sem_c, (0, c), over_col))
        start(("z", c), remote(source(c, mz, az), zr.at[rows_of(c)], sem_c, (1, c), over_col))

    def stage_row(c):
        live["z", c].wait_recv()
        rows = rows_of(c)
        xb[rows] = (source(c, mx, ax)[...] + zr[rows].astype(F32)).astype(BF16)
        start(("r", c), remote(xb.at[rows], xr.at[rows], sem_r, (c,), over_row))

    def stage_pair(c):
        live["y", c].wait_recv()
        live["r", c].wait_recv()
        rows = rows_of(c)
        sf[...] = source(c, mo, ao)[...] + yr[rows].astype(F32) + xr[rows].astype(F32)
        sb[rows] = sf[...].astype(BF16)
        tf[c] = sf[pl.ds(pl.multiple_of(parity * wide, wide), wide)]
        away = pl.ds(pl.multiple_of(c * size + (1 - parity) * wide, wide), wide)
        start(("p", c), remote(sb.at[away], pr.at[c], sem_p, (c,), pair))

    def stage_rest(c):
        live["p", c].wait_recv()
        tf[c] = tf[c] + pr[c].astype(F32)
        tb[c] = tf[c].astype(BF16)
        for k in range(1, peers):
            there = lax.rem(place + k, peers)
            piece = pl.ds(pl.multiple_of(there * block, block), block)
            start(
                ("q", c, k),
                remote(
                    tb.at[c, piece], qr.at[c, k], sem_z, (c, k), {"dp": 2 * there + parity}
                ),
            )

    def mine_of(c):
        at = c * size + parity * wide + place * block
        return pl.ds(pl.multiple_of(at, block), block)

    def stage_sum(c):
        total = tf[c, pl.ds(pl.multiple_of(place * block, block), block)]
        for k in range(1, peers):
            live["q", c, k].wait_recv()
            total = total + qr[c, k].astype(F32)
        out_ref[mine_of(c)] = total.astype(BF16)
        for k in range(1, peers):
            there = lax.rem(place + k, peers)
            start(
                ("g", c, k),
                remote(
                    out_ref.at[mine_of(c)], out_ref.at[mine_of(c)], sem_gz, (c, k),
                    {"dp": 2 * there + parity},
                ),
            )

    def stage_back(c):
        for k in range(1, peers):
            live["g", c, k].wait_recv()
        half = pl.ds(pl.multiple_of(c * size + parity * wide, wide), wide)
        start(("b", c), remote(out_ref.at[half], out_ref.at[half], sem_gp, (c,), pair))

    mine = row * cores + col
    theirs = (1 - row) * cores + col

    def begin_small():
        first = 2 * srow + scol
        start("s0", remote(s_ref.at[0:first], s_col, sem_s, (0,), over_col))

    def small_row():
        live["s0"].wait_recv()
        s_mid[0:srow] = s_ref[srow:2 * srow] + s_col[srow:2 * srow]
        s_mid[srow:srow + scol] = (
            s_ref[2 * srow + scol:2 * srow + 2 * scol] + s_col[2 * srow:2 * srow + scol]
        )
        start("s1", remote(s_mid, s_row, sem_s, (1,), over_row))

    def small_dp():
        live["s1"].wait_recv()
        s_dp[me, 0:srow] = s_ref[0:srow] + s_col[0:srow] + s_row[0:srow]
        s_dp[me, srow:srow + scol] = s_mid[srow:srow + scol] + s_row[srow:srow + scol]
        for k in range(1, n):
            peer = {"dp": lax.rem(me + k, n)}
            start(("s2", k), remote(s_dp.at[me], s_dp.at[me], sem_d, (k,), peer))

    def small_sum():
        for k in range(1, n):
            live["s2", k].wait_recv()
        acc = s_dp[0]
        for index in range(1, n):
            acc = acc + s_dp[index]
        sum_ref[...] = acc

    def begin_spread(i, own, away, out):
        start(("o0", i), remote(own, out.at[mine], sem_o, (i, 0), over_col))
        start(("o1", i), remote(away, out.at[mine], sem_o, (i, 1), over_row))
        out[mine] = own[...]

    def forward(i, out):
        live["o1", i].wait_recv()
        start(("o2", i), remote(out.at[theirs], out.at[theirs], sem_o, (i, 2), over_col))

    for c in range(chunks):
        begin(c)
    begin_small()
    stages = (stage_row, stage_pair, stage_rest, stage_sum, stage_back)
    for step in range(chunks + len(stages) - 1):
        for k in reversed(range(len(stages))):
            if 0 <= step - k < chunks:
                stages[k](step - k)
        if step == 0:
            small_row()
        if step == 1:
            small_dp()
        if step == 2:
            begin_spread(0, blk_own, blk_away, blk_out)
        if step == 3:
            begin_spread(1, in_own, in_away, in_out)
    forward(0, blk_out)
    forward(1, in_out)
    small_sum()
    for key, copy in live.items():
        copy.wait_send()
        if key[0] in ("b", "o0", "o2"):
            copy.wait_recv()


def group_total(n, mlp, att, small, srow, scol, block, rows_in, images):
    rows = mlp[0].shape[0] + att[0].shape[0]
    half = mlp[0].shape[1]
    size = max(n * 16, 256)
    chunks, peers, wide = rows // size, n // 2, size // 2
    dma = pltpu.SemaphoreType.DMA
    spread = jax.ShapeDtypeStruct((images,) + block[0].shape, BF16)
    args = (*mlp, *att, small, *block, *rows_in)
    return pl.pallas_call(
        functools.partial(total_kernel, n, size, srow, scol),
        name="group_total",
        out_shape=(
            jax.ShapeDtypeStruct((rows, half), BF16),
            jax.ShapeDtypeStruct((srow + scol, 128), F32),
            spread,
            spread,
        ),
        in_specs=[VMEM] * len(args),
        out_specs=(VMEM,) * 4,
        scratch_shapes=[pltpu.VMEM((rows, half), BF16)] * 4
        + [
            pltpu.VMEM((rows, half), BF16),
            pltpu.VMEM((size, half), F32),
            pltpu.VMEM((chunks, wide, half), BF16),
            pltpu.VMEM((chunks, wide, half), BF16),
            pltpu.VMEM((chunks, wide, half), F32),
            pltpu.VMEM((chunks, peers, size // n, half), BF16),
            pltpu.VMEM((2 * srow + scol, 128), F32),
            pltpu.VMEM((srow + scol, 128), F32),
            pltpu.VMEM((srow + scol, 128), F32),
            pltpu.VMEM((n, srow + scol, 128), F32),
            dma((2, 2, chunks)),
            dma((2, chunks)),
            dma((2, chunks)),
            dma((2, chunks, peers)),
            dma((2, chunks, peers)),
            dma((2, chunks)),
            dma((2, 2)),
            dma((2, n)),
            dma((2, 2, 3)),
        ],
        compiler_params=pltpu.CompilerParams(
            collective_id=0, has_side_effects=True, vmem_limit_bytes=LIMIT
        ),
    )(*args)


def local_call(kernel, shapes, scratch, flops, *args):
    return pl.pallas_call(
        kernel,
        out_shape=tuple(jax.ShapeDtypeStruct(shape, dtype) for shape, dtype in shapes),
        in_specs=[VMEM] * len(args),
        out_specs=tuple([VMEM] * len(shapes)),
        scratch_shapes=[pltpu.VMEM(shape, dtype) for shape, dtype in scratch],
        compiler_params=pltpu.CompilerParams(vmem_limit_bytes=LIMIT),
        cost_estimate=pl.CostEstimate(flops=flops, bytes_accessed=1 << 23, transcendentals=0),
    )(*args)


def per_device(
    block_input, out_grad, first_gain, first_shift, qkv_weight, query_bias, value_bias,
    position_table, position_index, proj_weight, proj_bias, second_gain, second_shift,
    expand_weight, expand_bias, reduce_weight, reduce_bias,
):
    n = lax.axis_size("dp")
    row, col = lax.axis_index("row"), lax.axis_index("col")
    cores = lax.axis_size("col")
    half = block_input.shape[1]
    width = qkv_weight.shape[2]
    hid = expand_weight.shape[1]
    heads = position_table.shape[1]
    entries = position_table.shape[0]
    images = block_input.shape[0] // IMAGE
    mine = row * cores + col
    theirs = (1 - row) * cores + col

    def image_of(tokens):
        shaped = tokens.reshape(images, IMAGE, half)
        own = lax.dynamic_index_in_dim(shaped, mine, 0, keepdims=False)
        away = lax.dynamic_index_in_dim(shaped, theirs, 0, keepdims=False)
        return own, away

    def lanes(vector):
        count = -(-vector.shape[0] // 1024) * 1024
        return jnp.pad(vector, (0, count - vector.shape[0])).reshape(-1, 128)

    x_own, x_away = image_of(block_input)
    g_own, g_away = image_of(out_grad)
    rows_own = jnp.stack(
        [first_gain, first_shift, proj_bias, second_gain, second_shift, reduce_bias]
        + [jnp.zeros_like(first_gain)] * 2
    )
    cols_own = jnp.concatenate(
        [query_bias, value_bias, expand_bias, position_table.reshape(-1)]
    )
    (x_oth, g_oth, rows_oth, cols_oth), (qkv, proj, expand, reduce) = gather(
        n, x_away, g_away, rows_own, lanes(cols_own), qkv_weight.reshape(half, 3 * width),
        proj_weight, expand_weight, reduce_weight,
    )
    rvec = jnp.concatenate([rows_own, rows_oth], axis=1)
    cols_oth = cols_oth.reshape(-1)[:cols_own.shape[0]]
    qb = jnp.concatenate([query_bias, cols_oth[:width]])[None]
    vb = jnp.concatenate([value_bias, cols_oth[width:2 * width]])[None]
    eb = jnp.concatenate([expand_bias, cols_oth[2 * width:2 * width + hid]])[None]
    table_oth = cols_oth[2 * width + hid:].reshape(entries, heads)
    table = jnp.concatenate([position_table, table_oth], axis=1)
    one_hot = (
        position_index.reshape(-1)[:, None] == jnp.arange(entries, dtype=jnp.int32)[None, :]
    ).astype(F32)
    bias = lax.dot_general(
        table, one_hot, (((0,), (1,)), ((), ())), precision=lax.Precision.HIGHEST
    ).reshape(2, heads, WINDOW, WINDOW)
    bias = jnp.pad(bias, ((0, 0), (0, 0), (0, PAD - WINDOW), (0, 0)))
    bias = jnp.pad(
        bias, ((0, 0), (0, 0), (0, 0), (0, PAD - WINDOW)), constant_values=-1e30
    ).reshape(2, heads * PAD, PAD)

    perm = jnp.asarray(permutation(), BF16)
    full, full_h, full_e = 2 * half, 2 * width, 2 * hid
    queries, keys, values, mixed, middle, x_rows = local_call(
        attend_kernel,
        [((ROWS, full_h), BF16)] * 4 + [((ROWS, full), F32), ((ROWS, full), BF16)],
        [],
        2 * ROWS * full * full_h * 6,
        perm, x_own, x_oth, rvec, qb, vb, bias, *qkv, *proj,
    )
    mlp_rows = hid // half * half + hid
    block, block_away, mgrad, m_o, m_x, m_y, m_z, m_rsum, eb_grad = local_call(
        mlp_kernel,
        [((IMAGE, half), BF16)] * 2 + [((ROWS, full), F32)]
        + [((mlp_rows, half), F32)] * 2
        + [((mlp_rows, half), BF16)] * 2
        + [((8, full), F32), ((1, full_e), F32)],
        [((ROWS, full_e), F32), ((ROWS, full_e), BF16), ((ROWS, full_e), BF16)],
        2 * ROWS * full * full_e * 6,
        perm, g_own, g_oth, rvec, eb, middle, *expand, *reduce,
    )

    att_rows = 3 * half + width
    in_rows, in_away, a_o, a_x, a_y, a_z, a_rsum, qv_grad, bgrad = local_call(
        back_kernel,
        [((IMAGE, half), BF16)] * 2
        + [((att_rows, half), F32)] * 2
        + [((att_rows, half), BF16)] * 2
        + [((8, full), F32), ((8, full_h), F32), ((2, heads * PAD, PAD), F32)],
        [((ROWS, full_h), BF16), ((ROWS, 3 * width), BF16)],
        2 * ROWS * full * full_h * 12,
        perm, x_rows, queries, keys, values, mixed, mgrad, rvec, bias, *qkv, *proj,
    )

    pairs = bgrad.reshape(2 * heads, PAD, PAD)[:, :WINDOW, :WINDOW].reshape(2 * heads, -1)
    table_grad = lax.dot_general(
        one_hot, pairs, (((0,), (1,)), ((), ())), precision=lax.Precision.HIGHEST
    )
    row_sums = jnp.concatenate([a_rsum[0:2], m_rsum[0:4]])
    row_o, row_x = row_sums[:, :half].reshape(-1), row_sums[:, half:].reshape(-1)

    def col_pack(b):
        return jnp.concatenate(
            [
                qv_grad[0, b * width:(b + 1) * width],
                qv_grad[1, b * width:(b + 1) * width],
                eb_grad[0, b * hid:(b + 1) * hid],
                table_grad[:, b * heads:(b + 1) * heads].reshape(-1),
            ]
        )

    size = row_o.shape[0]

    row_o, row_x, col_o, col_x = lanes(row_o), lanes(row_x), lanes(col_pack(0)), lanes(col_pack(1))
    srow, scol = row_o.shape[0], col_o.shape[0]
    grads, sums, block_output, input_grad = group_total(
        n, (m_o, m_x, m_y, m_z), (a_o, a_x, a_y, a_z),
        jnp.concatenate([row_o, row_x, col_x, col_o]), srow, scol,
        (block, block_away), (in_rows, in_away), images,
    )
    block_output = block_output.reshape(images * IMAGE, half)
    input_grad = input_grad.astype(F32).reshape(images * IMAGE, half)
    grads = grads.astype(F32)
    sums = sums.reshape(-1)
    expand_g = (
        grads[:hid].reshape(hid // half, half, half).transpose(1, 0, 2).reshape(half, hid)
    )
    reduce_g = grads[hid:2 * hid]
    qkv_g = grads[2 * hid:2 * hid + 3 * half].reshape(3, half, width).transpose(1, 0, 2)
    proj_g = grads[2 * hid + 3 * half:]
    first_gain_g, first_shift_g, proj_b_g, second_gain_g, second_shift_g, reduce_b_g = (
        sums[i * half:(i + 1) * half] for i in range(6)
    )
    rest = sums[srow * 128:]
    return (
        block_output,
        input_grad,
        first_gain_g,
        first_shift_g,
        qkv_g,
        rest[:width],
        rest[width:2 * width],
        rest[2 * width + hid:2 * width + hid + entries * heads].reshape(entries, heads),
        proj_g,
        proj_b_g,
        second_gain_g,
        second_shift_g,
        expand_g,
        rest[2 * width:2 * width + hid],
        reduce_g,
        reduce_b_g,
    )


def solution(mesh):
    in_specs = (
        P("dp", "row"), P("dp", "row"), P("row"), P("row"), P("row", None, "col"), P("col"),
        P("col"), P(None, "col"), P(), P("col", "row"), P("row"), P("row"), P("row"),
        P("row", "col"), P("col"), P("col", "row"), P("row"),
    )
    out_specs = (
        P("dp", "row"), P("dp", "row"), P("row"), P("row"), P("row", None, "col"), P("col"),
        P("col"), P(None, "col"), P("col", "row"), P("row"), P("row"), P("row"),
        P("row", "col"), P("col"), P("col", "row"), P("row"),
    )
    return jax.shard_map(
        per_device, mesh=mesh, in_specs=in_specs, out_specs=out_specs, check_vma=False
    )
```
